32 devices in a mesh: grp: 2 (over y), dec: 4 (over z), stg: 2 (over x), tp: 2 (over core).
Axes of the slice: x: 2, y: 2, z: 4, core: 2. Of those that a mesh axis runs over, the one named last changes fastest.
Arguments:
- hidden_x: bfloat16 [3072, 7168], P(('grp', 'dec'), ('stg', 'tp')), parts along dimension 0, may hold values from -8 to 8
- proj_weight: bfloat16 [7168, 2112], P(('stg', 'tp'), 'dec'), may hold values from -0.0625 to 0.0625
- q_gain: float32 [1536], replicated, may hold values from 0.25 to 1.75
- kv_gain: float32 [512], replicated, may hold values from 0.25 to 1.75
- old_cache: bfloat16 [256, 32, 576], P(('grp', 'dec')), parts along dimension 0, may hold values from -6 to 6
- page_plan: int32 [96, 2], P(('grp', 'dec')), parts along dimension 0, may hold values from 0 to 31, as said below
- block_table: int32 [8, 4, 8], P(('grp', 'dec')), parts along dimension 0, may hold values from 0 to 31, as said below
- split_lens: int32 [8, 4], P('grp', 'dec'), parts along dimension 0, may hold values from 2 to 256, as said below
- dec_query: bfloat16 [8, 128, 576], P('grp', ('stg', 'tp')), parts along dimension 0, may hold values from -66 to 66
- new_key: bfloat16 [8, 576], P('grp'), parts along dimension 0, may hold values from -12 to 12
Outputs:
- q_latent: bfloat16 [3072, 1536], P(('grp', 'dec'), ('stg', 'tp')), parts along dimension 0
- attn_latent: bfloat16 [8, 128, 512], P('grp', ('stg', 'tp')), parts along dimension 0
The draws below stay inside these ranges and needn't reach their ends.
There are 2 independent parts, one for each index of `grp`. The reference program is written for one: setup_inputs(seed, part) draws one part's arguments, and reference() takes and returns one part's arrays. A program takes and returns all parts, laid end to end along the dimension named above; an argument that names none is the same for every part. Nothing has to cross between parts.
Inputs may be any that keep to these rules, and one draw needn't show every extreme that they name: `page_plan`: column 0 is the owner of prefill page g, column 1 its slot among the owner's 32; no two pages share owner and slot; in each aligned block of 12 rows (one index of dec) no owner appears more than 3 times and some owner exactly 3 times; no page goes to a slot block_table[o, r, 0]. `block_table`: for each owner the 4 x 8 entries are its 32 slots, each once. `split_lens`: each request has exactly 256 tokens on at least one owner.
All inputs are finite; a program needn't handle non-finite values.
Results may differ from the reference program's by a relative error of at most 0.0054.
Values may be sent and summed in bfloat16 or wider, within the bound.
A program may use at most 64 MiB of HBM per device.

```python
import jax
import jax.numpy as jnp
from jax import lax

D = 7168
QL = 1536
KVL = 512
ROPE = 64
H = 128
PAGE = 32
REQS = 4
PPR = 8
KVW = 576
PROJ = 2112
TOKENS = 1536
PPS = 12
NPG = 48
CAPP = 3
GROUPS = 4
SLOTS = 32
N_DEC = 4


def plan_tables(key):
    shuffle = jax.random.permutation(jax.random.fold_in(key, 11), N_DEC)

    def block_owners(source):
        shuffled = jax.random.permutation(jax.random.fold_in(jax.random.fold_in(key, 12), source), PPS)
        return shuffle[(source * GROUPS + shuffled // CAPP) % N_DEC]
    owners = jax.vmap(block_owners)(jnp.arange(N_DEC, dtype=jnp.int32)).reshape(NPG)
    onehot = (owners[:, None] == jnp.arange(N_DEC, dtype=jnp.int32)[None, :]).astype(jnp.int32)
    before = jnp.cumsum(onehot, axis=0) - onehot
    arrival = jnp.sum(before * onehot, axis=1)

    def owner_slots(owner):
        return jax.random.permutation(jax.random.fold_in(jax.random.fold_in(key, 13), owner), SLOTS)
    slot_orders = jax.vmap(owner_slots)(jnp.arange(N_DEC, dtype=jnp.int32))
    plan_slots = slot_orders[owners, REQS + arrival]
    page_table = jnp.stack([owners, plan_slots], axis=1).astype(jnp.int32)
    slot_table = jnp.transpose(slot_orders.reshape(N_DEC, PPR, REQS), (0, 2, 1)).astype(jnp.int32)
    longest = PPR * PAGE
    spread = longest - 1
    draw_first = jax.random.randint(jax.random.fold_in(key, 14), (REQS, N_DEC), 0, spread)
    draw_second = jax.random.randint(jax.random.fold_in(key, 15), (REQS, N_DEC), 0, spread)
    length_table = longest - draw_first * draw_second // spread
    longest_owner = jax.random.randint(jax.random.fold_in(key, 16), (REQS,), 0, N_DEC)
    length_table = jnp.where(jnp.arange(N_DEC, dtype=jnp.int32)[None, :] == longest_owner[:, None], longest, length_table)
    return (page_table, slot_table, length_table.astype(jnp.int32))


def draw_page_plan(key, part):
    return plan_tables(key)[0]


def draw_block_table(key, part):
    return plan_tables(key)[1]


def draw_split_lens(key, part):
    return plan_tables(key)[2]


def draw_old_cache(key, part):
    extent = (N_DEC * SLOTS, PAGE, KVW)
    values_out = jnp.clip(jax.random.normal(jax.random.fold_in(key, 21), extent, jnp.float32), -6.0, 6.0)
    return values_out.astype(jnp.bfloat16)


def draw_dec_query(key, part):
    extent = (REQS, H, KVW)
    values_out = jnp.clip(1.5 * jax.random.normal(jax.random.fold_in(key, 31), extent, jnp.float32), -9.0, 9.0)
    return values_out.astype(jnp.bfloat16)


def draw_hidden_x(key, part):
    extent = (TOKENS, D)
    baseline = jnp.clip(jax.random.normal(jax.random.fold_in(key, 41), extent, jnp.float32), -4.0, 4.0)
    row_scale = jnp.exp(jax.random.uniform(jax.random.fold_in(key, 42), (TOKENS,), jnp.float32, -0.69, 0.69))
    return (baseline * row_scale[:, None]).astype(jnp.bfloat16)


def steps_of(stream_key, shape, shards, low, largest):
    level, own = 1.0, jax.random.fold_in(stream_key, 6)
    for dim, shards_of in shards:
        steps = jnp.exp(jax.random.uniform(jax.random.fold_in(own, dim), (shards_of,), jnp.float32, low / len(shards), largest / len(shards)))
        level = level * jnp.repeat(steps, shape[dim] // shards_of).reshape([-1 if axis == dim else 1 for axis in range(len(shape))])
    return level


def gaussian(key, dims, scale, most, shards=(), kind=jnp.bfloat16):
    array = jax.random.normal(key, dims, jnp.float32) * scale
    if len(shards) > 0:
        array = steps_of(key, dims, shards, -0.22, 0.18) * array
    return jnp.clip(array, min=-most, max=most).astype(kind)


def setup_inputs(seed: int = 0, part: int = 0) -> dict:
    arg_keys = jax.random.split(jax.random.key(seed), 11)
    own_keys = jax.random.split(jax.random.fold_in(arg_keys[10], part), 11)
    hidden_x = draw_hidden_x(jax.random.fold_in(jax.random.fold_in(arg_keys[10], part), 71), part)
    proj_weight = gaussian(arg_keys[1], (D, PROJ), D ** -0.5, 0.0625, ((0, 4), (1, 4)))
    q_gain = jnp.clip(1.0 + 0.15 * jax.random.normal(arg_keys[2], (QL,), jnp.float32), 0.25, 1.75)
    kv_gain = jnp.clip(1.0 + 0.15 * jax.random.normal(arg_keys[3], (KVL,), jnp.float32), 0.25, 1.75)
    old_cache = draw_old_cache(jax.random.fold_in(jax.random.fold_in(arg_keys[10], part), 71), part)
    page_plan = draw_page_plan(jax.random.fold_in(jax.random.fold_in(arg_keys[10], part), 71), part)
    block_table = draw_block_table(jax.random.fold_in(jax.random.fold_in(arg_keys[10], part), 71), part)
    split_lens = draw_split_lens(jax.random.fold_in(jax.random.fold_in(arg_keys[10], part), 71), part)
    dec_query = draw_dec_query(jax.random.fold_in(jax.random.fold_in(arg_keys[10], part), 71), part)
    new_key = gaussian(own_keys[9], (REQS, KVW), 2.0, 12.0)
    return {"hidden_x": hidden_x, "proj_weight": proj_weight, "q_gain": q_gain, "kv_gain": kv_gain, "old_cache": old_cache, "page_plan": page_plan, "block_table": block_table, "split_lens": split_lens, "dec_query": dec_query, "new_key": new_key}


softmax_scale = 192.0 ** (-0.5)
norm_eps = 1e-06

def rope_rotate(matrix, col_start, positions):
    col_count = matrix.shape[1]
    columns = col_start + jnp.arange(col_count, dtype=jnp.int32)
    is_rope = columns >= KVL
    pair_index = jnp.maximum(columns - KVL, 0) // 2
    frequency = jnp.power(jnp.float32(10000.0), -(2 * pair_index).astype(jnp.float32) / ROPE)
    angles = positions[:, None] * frequency[None, :]
    cosine = jnp.where(is_rope[None, :], jnp.cos(angles), 1.0)
    sine_part = jnp.where(is_rope[None, :], jnp.sin(angles), 0.0)
    paired = matrix.reshape(matrix.shape[0], col_count // 2, 2)
    partner = jnp.stack([-paired[:, :, 1], paired[:, :, 0]], axis=2).reshape(matrix.shape)
    return matrix * cosine + partner * sine_part

def kv_finish(matrix, col_start, latent_sq, kv_gain, positions):
    col_count = matrix.shape[1]
    columns = col_start + jnp.arange(col_count, dtype=jnp.int32)
    gain_full = jnp.concatenate([kv_gain, jnp.ones((ROPE,), jnp.float32)])
    gain_cols = lax.dynamic_slice_in_dim(gain_full, col_start, col_count)
    inverse = lax.rsqrt(latent_sq / KVL + norm_eps)
    row_scale = jnp.where(columns[None, :] < KVL, inverse[:, None] * gain_cols[None, :], 1.0)
    return rope_rotate(matrix * row_scale, col_start, positions).astype(jnp.bfloat16)

def reference(hidden_x, proj_weight, q_gain, kv_gain, old_cache, page_plan, block_table, split_lens, dec_query, new_key):
    projected = jnp.dot(hidden_x, proj_weight, preferred_element_type=jnp.float32)
    query_part = projected[:, :QL]
    query_sq = lax.optimization_barrier(jnp.sum(query_part * query_part, axis=1))
    q_latent = (query_part * lax.rsqrt(query_sq / QL + norm_eps)[:, None] * q_gain[None, :]).astype(jnp.bfloat16)
    kv_part = projected[:, QL:]
    latent_sq = lax.optimization_barrier(jnp.sum(kv_part[:, :KVL] * kv_part[:, :KVL], axis=1))
    positions = jnp.arange(TOKENS, dtype=jnp.int32).astype(jnp.float32)
    new_rows = kv_finish(kv_part, 0, latent_sq, kv_gain, positions)
    new_pages = new_rows.reshape(NPG, PAGE, KVW)
    targets = page_plan[:, 0] * SLOTS + page_plan[:, 1]
    cache = old_cache.at[targets].set(new_pages)
    query = dec_query.astype(jnp.float32)

    def owner_partial(owner):
        slot_rows = block_table[owner]
        key_rows = cache[owner * SLOTS + slot_rows].reshape(REQS, PPR * PAGE, KVW).astype(jnp.float32)
        scores = jnp.einsum('rhc,rlc->rhl', query, key_rows) * softmax_scale
        live_mask = jnp.arange(PPR * PAGE, dtype=jnp.int32)[None, :] < split_lens[:, owner][:, None]
        scores = jnp.where(live_mask[:, None, :], scores, -1e+30)
        row_peak = lax.optimization_barrier(jnp.max(scores, axis=2))
        weights = jnp.where(live_mask[:, None, :], jnp.exp(scores - row_peak[:, :, None]), 0.0)
        row_total = lax.optimization_barrier(jnp.sum(weights, axis=2))
        rounded = lax.optimization_barrier(weights.astype(jnp.bfloat16)).astype(jnp.float32)
        partial_out = jnp.einsum('rhl,rlc->rhc', rounded, key_rows[:, :, :KVL])
        return (row_peak, row_total, partial_out)
    peaks, totals, partials = lax.map(owner_partial, jnp.arange(N_DEC, dtype=jnp.int32))
    self_score = jnp.einsum('rhc,rc->rh', query, new_key.astype(jnp.float32)) * softmax_scale
    overall = jnp.maximum(lax.optimization_barrier(jnp.max(peaks, axis=0)), self_score)
    factor = jnp.exp(peaks - overall[None])
    self_weight = jnp.exp(self_score - overall)
    denom = lax.optimization_barrier(jnp.sum(totals * factor, axis=0)) + self_weight
    numer = lax.optimization_barrier(jnp.sum(partials * factor[..., None], axis=0)) + self_weight[..., None] * new_key[:, None, :KVL].astype(jnp.float32)
    attn_latent = (numer / denom[..., None]).astype(jnp.bfloat16)
    return (q_latent, attn_latent)
```

```python
import functools

import jax
import jax.numpy as jnp
from jax import lax
from jax.experimental import pallas as pl
from jax.experimental.pallas import tpu as pltpu
from jax.sharding import PartitionSpec as P

QL = 1536
KVL = 512
ROPE = 64
PAGE = 32


softmax_scale = 192.0 ** (-0.5)
norm_eps = 1e-06


def combined_all(part, axis, combine):
    gathered = jax.tree.map(lambda a: lax.all_gather(a, axis), part)

    def take(source):
        return jax.tree.map(lambda a: lax.dynamic_index_in_dim(a, source, 0, False), gathered)

    return lax.fori_loop(
        1, lax.axis_size(axis), lambda source, state: combine(state, take(source)), take(0)
    )


def rope_rotate(matrix, col_start, positions):
    col_count = matrix.shape[1]
    columns = col_start + jnp.arange(col_count, dtype=jnp.int32)
    is_rope = columns >= KVL
    pair_index = jnp.maximum(columns - KVL, 0) // 2
    frequency = jnp.power(jnp.float32(10000.0), -(2 * pair_index).astype(jnp.float32) / ROPE)
    angles = positions[:, None] * frequency[None, :]
    cosine = jnp.where(is_rope[None, :], jnp.cos(angles), 1.0)
    sine_part = jnp.where(is_rope[None, :], jnp.sin(angles), 0.0)
    paired = matrix.reshape(matrix.shape[0], col_count // 2, 2)
    partner = jnp.stack([-paired[:, :, 1], paired[:, :, 0]], axis=2).reshape(matrix.shape)
    return matrix * cosine + partner * sine_part


def kv_finish(matrix, col_start, latent_sq, kv_gain, positions):
    col_count = matrix.shape[1]
    columns = col_start + jnp.arange(col_count, dtype=jnp.int32)
    gain_full = jnp.concatenate([kv_gain, jnp.ones((ROPE,), jnp.float32)])
    gain_cols = lax.dynamic_slice_in_dim(gain_full, col_start, col_count)
    inverse = lax.rsqrt(latent_sq / KVL + norm_eps)
    row_scale = jnp.where(columns[None, :] < KVL, inverse[:, None] * gain_cols[None, :], 1.0)
    return rope_rotate(matrix * row_scale, col_start, positions).astype(jnp.bfloat16)


def pack_pages(kv_pages, page_table, owner_count, capacity):
    owners = page_table[:, 0]
    slot_ids = page_table[:, 1]
    page_ids = jnp.arange(kv_pages.shape[0], dtype=jnp.int32)
    earlier = (owners[:, None] == owners[None, :]) & (page_ids[None, :] < page_ids[:, None])
    ranking = jnp.sum(earlier.astype(jnp.int32), axis=1)
    targets = owners * capacity + ranking
    places = jnp.arange(owner_count * capacity, dtype=jnp.int32)
    matches = targets[None, :] == places[:, None]
    source_ids = jnp.sum(jnp.where(matches, page_ids[None, :], 0), axis=1)
    filled = jnp.any(matches, axis=1)
    chosen = jnp.where(
        filled[:, None, None], jnp.take(kv_pages, source_ids, axis=0), jnp.zeros((), kv_pages.dtype)
    )
    labels = jnp.where(filled, jnp.take(slot_ids, source_ids), -1).astype(jnp.bfloat16)
    return (
        chosen.reshape(owner_count, capacity, kv_pages.shape[1], kv_pages.shape[2]),
        labels.reshape(owner_count, capacity),
    )


def place_pages(old_cache, got_pages, got_labels):
    flat_pages = got_pages.reshape(-1, old_cache.shape[1], old_cache.shape[2])
    label_ids = got_labels.reshape(-1).astype(jnp.int32)
    slot_ids = jnp.arange(old_cache.shape[0], dtype=jnp.int32)
    arrival_ids = jnp.arange(label_ids.shape[0], dtype=jnp.int32)
    matches = label_ids[None, :] == slot_ids[:, None]
    source_ids = jnp.sum(jnp.where(matches, arrival_ids[None, :], 0), axis=1)
    arrived = jnp.any(matches, axis=1)
    return jnp.where(arrived[:, None, None], jnp.take(flat_pages, source_ids, axis=0), old_cache)


def combine_parts(former, latter):
    overall = jnp.maximum(former[0], latter[0])
    front_scale = jnp.exp(former[0] - overall)
    back_scale = jnp.exp(latter[0] - overall)
    return (
        overall,
        former[1] * front_scale + latter[1] * back_scale,
        former[2] * front_scale[:, :, None] + latter[2] * back_scale[:, :, None],
    )


MESH = pl.DeviceIdType.MESH


def proj_kernel(
    dims, w_ref, x_ref, qg_ref, kg_ref, cos_ref, sin_ref, q_out, k_out,
    wbuf, pt, aq, bq, bk, cq, ck, eq, ek, ss, ssin,
    zsem, zrecv, ysem, yrecv, t_send, t_recv, s_send, s_recv, v_send, v_recv,
):
    D, G, S, T, K = dims
    C, fg = w_ref.shape[1], w_ref.shape[2]
    qw, kw = qg_ref.shape[0], kg_ref.shape[0]
    ck_rows = C // K
    me, g = lax.axis_index("dec"), lax.axis_index("grp")
    st, tp = lax.axis_index("stg"), lax.axis_index("tp")

    barrier = pltpu.get_barrier_semaphore()

    def greet(target):
        pl.semaphore_signal(barrier, inc=1, device_id=target, device_id_type=MESH)

    @pl.when(me > 0)
    def _():
        greet({"dec": me - 1})

    @pl.when(me < D - 1)
    def _():
        greet({"dec": me + 1})

    for d in range(1, G):
        greet({"grp": lax.rem(g + d, G)})
    lane_steps = [(a, b) for a in range(S) for b in range(T) if a or b]

    def lane_at(a, b):
        return {"stg": lax.rem(st + a, S), "tp": lax.rem(tp + b, T)}

    for a, b in lane_steps:
        greet(lane_at(a, b))
    ends = (me > 0).astype(jnp.int32) + (me < D - 1).astype(jnp.int32)
    pl.semaphore_wait(barrier, ends + (G - 1) + len(lane_steps))

    def chunk(ref, j, part, c):
        return ref.at[j, part, pl.ds(c * ck_rows, ck_rows)]

    def z_copy(j, c, way, own):
        src = w_ref.at[g, pl.ds(c * ck_rows, ck_rows)] if own else chunk(wbuf, j, g, c)
        to = me + 1 if way == 0 else me - 1
        return pltpu.make_async_remote_copy(
            src_ref=src, dst_ref=chunk(wbuf, j, g, c),
            send_sem=zsem.at[way, j, c], recv_sem=zrecv.at[j, c],
            device_id={"dec": to}, device_id_type=MESH,
        )

    def y_copy(j, c, d):
        return pltpu.make_async_remote_copy(
            src_ref=chunk(wbuf, j, g, c), dst_ref=chunk(wbuf, j, g, c),
            send_sem=ysem.at[d - 1, j, c], recv_sem=yrecv.at[d - 1, j, c],
            device_id={"grp": lax.rem(g + d, G)}, device_id_type=MESH,
        )

    def y_arrive(j, c, d):
        part = lax.rem(g + G - d, G)
        return pltpu.make_async_remote_copy(
            src_ref=chunk(wbuf, j, part, c), dst_ref=chunk(wbuf, j, part, c),
            send_sem=ysem.at[d - 1, j, c], recv_sem=yrecv.at[d - 1, j, c],
            device_id={"grp": part}, device_id_type=MESH,
        )

    def can_send(way):
        return me < D - 1 if way == 0 else me > 0

    def sides(s):
        left, right = me - s, me + s
        return ((0, left, left >= 0), (1, right, right <= D - 1))

    for c in range(K):
        for way in (0, 1):
            @pl.when(can_send(way))
            def _():
                z_copy(me, c, way, True).start()

    def project(weights, j):
        total = None
        for part in range(G):
            term = lax.dot_general(
                weights(part), x_ref[:, part * fg : (part + 1) * fg],
                (((1,), (1,)), ((), ())), preferred_element_type=jnp.float32,
            )
            total = term if total is None else total + term
        pt[pl.ds(pl.multiple_of(j * C, 16), C), :] = total

    project(lambda part: w_ref[part], me)

    def finish_round(s):
        for way, j, there in sides(s):
            @pl.when(there)
            def _():
                for c in range(K):
                    for d in range(1, G):
                        y_arrive(j, c, d).wait_recv()
                project(lambda part: wbuf[j, part], j)

    for s in range(1, D):
        for c in range(K):
            for way, j, there in sides(s):
                @pl.when(there)
                def _():
                    z_copy(j, c, way, False).wait_recv()
                    for d in range(1, G):
                        y_copy(j, c, d).start()

                @pl.when(there & can_send(way))
                def _():
                    z_copy(j, c, way, False).start()
        if s > 1:
            finish_round(s - 1)
    finish_round(D - 1)

    def q_rows(lane):
        return pt[pl.ds(pl.multiple_of(lane * qw, 16), qw), :]

    def k_view(lane):
        return pt.at[pl.ds(pl.multiple_of(QL + lane * kw, 16), kw)]

    copies = []
    for d in range(1, T):
        t2 = lax.rem(tp + d, T)
        for a in range(S):
            kcopy = pltpu.make_async_remote_copy(
                src_ref=k_view(a * T + t2), dst_ref=bk.at[d - 1, a],
                send_sem=t_send.at[0, d - 1, a], recv_sem=t_recv.at[0, d - 1, a],
                device_id={"tp": t2}, device_id_type=MESH,
            )
            kcopy.start()
            aq[d - 1, a] = q_rows(a * T + t2).astype(jnp.bfloat16)
            qcopy = pltpu.make_async_remote_copy(
                src_ref=aq.at[d - 1, a], dst_ref=bq.at[d - 1, a],
                send_sem=t_send.at[1, d - 1, a], recv_sem=t_recv.at[1, d - 1, a],
                device_id={"tp": t2}, device_id_type=MESH,
            )
            qcopy.start()
            copies += [kcopy, qcopy]
    for copy in copies:
        copy.wait_recv()

    def tp_sum(a):
        lane = a * T + tp
        q, k = q_rows(lane), k_view(lane)[...]
        for d in range(T - 1):
            q = q + bq[d, a].astype(jnp.float32)
            k = k + bk[d, a]
        return q, k

    far = []
    for d in range(1, S):
        s2 = lax.rem(st + d, S)
        q, k = tp_sum(s2)
        ck[d - 1] = k
        cq[d - 1] = q.astype(jnp.bfloat16)
        for kind, (src, dst) in enumerate(((ck, ek), (cq, eq))):
            copy = pltpu.make_async_remote_copy(
                src_ref=src.at[d - 1], dst_ref=dst.at[d - 1],
                send_sem=s_send.at[kind, d - 1], recv_sem=s_recv.at[kind, d - 1],
                device_id={"stg": s2}, device_id_type=MESH,
            )
            copy.start()
            far.append(copy)
    q, k = tp_sum(st)
    for copy in far:
        copy.wait_recv()
    for d in range(S - 1):
        q = q + eq[d].astype(jnp.float32)
        k = k + ek[d]
    cols = (st * T + tp) * kw + lax.broadcasted_iota(jnp.int32, k.shape, 0)
    latent = cols < KVL
    ss[0:1, :] = jnp.sum(q * q, axis=0, keepdims=True)
    ss[1:2, :] = jnp.sum(jnp.where(latent, k * k, 0.0), axis=0, keepdims=True)
    small = []
    for i, (a, b) in enumerate(lane_steps):
        copy = pltpu.make_async_remote_copy(
            src_ref=ss, dst_ref=ssin.at[i], send_sem=v_send.at[i], recv_sem=v_recv.at[i],
            device_id=lane_at(a, b), device_id_type=MESH,
        )
        copy.start()
        small.append(copy)
    sq = ss[...]
    for i, copy in enumerate(small):
        copy.wait_recv()
        sq = sq + ssin[i]
    qn = q * lax.rsqrt(sq[0:1] / QL + norm_eps) * qg_ref[...]
    q_out[...] = jnp.transpose(qn).astype(jnp.bfloat16)
    kn = k * jnp.where(latent, lax.rsqrt(sq[1:2] / KVL + norm_eps) * kg_ref[...], 1.0)
    even = lax.rem(lax.broadcasted_iota(jnp.int32, k.shape, 0), 2) == 0
    partner = jnp.where(even, -pltpu.roll(kn, kw - 1, 0), pltpu.roll(kn, 1, 0))
    k_out[...] = (kn * cos_ref[...] + partner * sin_ref[...]).astype(jnp.bfloat16)

    for copy in copies + far + small:
        copy.wait_send()
    for s in range(D):
        for c in range(K):
            for way, j, there in sides(s):
                @pl.when(there & can_send(way))
                def _():
                    z_copy(j, c, way, s == 0).wait_send()

                if s > 0:
                    @pl.when(there)
                    def _():
                        for d in range(1, G):
                            y_copy(j, c, d).wait_send()


def chunk_count(rows):
    return next(k for k in (3, 2, 1) if rows % (16 * k) == 0)


def fused_ok(hidden_x, proj_weight):
    sizes = [lax.axis_size(n) for n in ("dec", "grp", "stg", "tp")]
    lanes = sizes[2] * sizes[3]
    return (
        proj_weight.shape[1] % 16 == 0
        and hidden_x.shape[0] % 128 == 0
        and hidden_x.shape[1] % (128 * sizes[1]) == 0
        and QL % (16 * lanes) == 0
        and (KVL + ROPE) % (16 * lanes) == 0
    )


def fused_projection(hidden_x, proj_weight, q_gain, kv_gain, positions):
    D, G, S, T = [lax.axis_size(n) for n in ("dec", "grp", "stg", "tp")]
    L = S * T
    rows, features = hidden_x.shape
    C = proj_weight.shape[1]
    K = chunk_count(C)
    fg, qw, kw = features // G, QL // L, (KVL + ROPE) // L
    lane = lax.axis_index(("stg", "tp"))
    weight = jnp.transpose(proj_weight.reshape(G, fg, C), (0, 2, 1))
    qg = lax.dynamic_slice_in_dim(q_gain, lane * qw, qw)[:, None]
    gain_full = jnp.concatenate([kv_gain, jnp.ones((ROPE,), jnp.float32)])
    kg = lax.dynamic_slice_in_dim(gain_full, lane * kw, kw)[:, None]
    columns = lane * kw + jnp.arange(kw, dtype=jnp.int32)
    is_rope = (columns >= KVL)[:, None]
    pair_index = jnp.maximum(columns - KVL, 0) // 2
    frequency = jnp.power(jnp.float32(10000.0), -(2 * pair_index).astype(jnp.float32) / ROPE)
    angles = frequency[:, None] * positions[None, :]
    cosine = jnp.where(is_rope, jnp.cos(angles), 1.0)
    sine = jnp.where(is_rope, jnp.sin(angles), 0.0)
    dma = pltpu.SemaphoreType.DMA
    bf, f32 = jnp.bfloat16, jnp.float32
    t1, s1, g1 = max(T - 1, 1), max(S - 1, 1), max(G - 1, 1)
    q_out, k_out = pl.pallas_call(
        functools.partial(proj_kernel, (D, G, S, T, K)),
        out_shape=(
            jax.ShapeDtypeStruct((rows, qw), bf),
            jax.ShapeDtypeStruct((kw, rows), bf),
        ),
        in_specs=[pl.BlockSpec(memory_space=pltpu.VMEM)] * 6,
        out_specs=(pl.BlockSpec(memory_space=pltpu.VMEM),) * 2,
        scratch_shapes=[
            pltpu.VMEM((D, G, C, fg), bf),
            pltpu.VMEM((D * C, rows), f32),
            pltpu.VMEM((t1, S, qw, rows), bf),
            pltpu.VMEM((t1, S, qw, rows), bf),
            pltpu.VMEM((t1, S, kw, rows), f32),
            pltpu.VMEM((s1, qw, rows), bf),
            pltpu.VMEM((s1, kw, rows), f32),
            pltpu.VMEM((s1, qw, rows), bf),
            pltpu.VMEM((s1, kw, rows), f32),
            pltpu.VMEM((8, rows), f32),
            pltpu.VMEM((max(L - 1, 1), 8, rows), f32),
            dma((2, D, K)), dma((D, K)), dma((g1, D, K)), dma((g1, D, K)),
            dma((2, t1, S)), dma((2, t1, S)), dma((2, s1)), dma((2, s1)),
            dma((max(L - 1, 1),)), dma((max(L - 1, 1),)),
        ],
        compiler_params=pltpu.CompilerParams(
            collective_id=0, has_side_effects=True, vmem_limit_bytes=48 * 1024 * 1024
        ),
    )(weight, hidden_x, qg, kg, cosine, sine)
    return q_out, jnp.transpose(k_out)


def body(
    hidden_x,
    proj_weight,
    q_gain,
    kv_gain,
    old_cache,
    page_plan,
    block_table,
    split_lens,
    dec_query,
    new_key,
):
    tokens_here = hidden_x.shape[0]
    positions = (
        lax.axis_index("dec") * tokens_here + jnp.arange(tokens_here, dtype=jnp.int32)
    ).astype(jnp.float32)
    lane_count = lax.axis_size(("stg", "tp"))
    lane_index = lax.axis_index(("stg", "tp"))
    owner_count = lax.axis_size("dec")
    page_count = page_plan.shape[0]
    capacity = max(2, -(-page_count // owner_count))
    query_width = QL // lane_count
    if fused_ok(hidden_x, proj_weight):
        q_latent, kv_rows = fused_projection(hidden_x, proj_weight, q_gain, kv_gain, positions)
    else:
        projected = jnp.dot(
            hidden_x,
            lax.all_gather(proj_weight, "dec", axis=1, tiled=True),
            preferred_element_type=jnp.float32,
        )
        query_part = projected[:, :QL]
        kv_part = projected[:, QL:]
        query_cols, kv_cols = (
            lax.psum_scatter(query_part, ("stg", "tp"), scatter_dimension=1, tiled=True),
            lax.psum_scatter(kv_part, ("stg", "tp"), scatter_dimension=1, tiled=True),
        )
        kv_width = kv_cols.shape[1]
        col_start = lane_index * kv_width
        columns = col_start + jnp.arange(kv_width, dtype=jnp.int32)
        latent_part_sq = jnp.sum(jnp.where(columns[None, :] < KVL, kv_cols * kv_cols, 0.0), axis=1)
        query_sq, latent_sq = lax.psum(
            (jnp.sum(query_cols * query_cols, axis=1), latent_part_sq), ("stg", "tp")
        )
        kv_rows = kv_finish(kv_cols, col_start, latent_sq, kv_gain, positions)
        query_gain = lax.dynamic_slice_in_dim(q_gain, lane_index * query_width, query_width)
        q_latent = (
            query_cols * lax.rsqrt(query_sq / QL + norm_eps)[:, None] * query_gain[None, :]
        ).astype(jnp.bfloat16)
    kv_width = kv_rows.shape[1]
    kv_pages = kv_rows.reshape(page_count, PAGE, kv_width)
    send_pages, send_labels = pack_pages(kv_pages, page_plan, owner_count, capacity)
    got_slices, got_labels = (
        lax.all_to_all(send_pages, "dec", split_axis=0, concat_axis=0, tiled=True),
        lax.all_to_all(send_labels, "dec", split_axis=0, concat_axis=0, tiled=True),
    )
    got_pages = lax.all_gather(got_slices, ("stg", "tp"), axis=3, tiled=True)
    cache = place_pages(old_cache, got_pages, got_labels)
    slot_table = block_table[0]
    request_count = slot_table.shape[0]
    key_rows = jnp.take(cache, slot_table.reshape(-1), axis=0).reshape(
        request_count, -1, cache.shape[2]
    )
    scores = (
        jnp.einsum("rhc,rlc->rhl", dec_query, key_rows, preferred_element_type=jnp.float32)
        * softmax_scale
    )
    live_mask = jnp.arange(key_rows.shape[1], dtype=jnp.int32)[None, :] < split_lens[:, 0][:, None]
    scores = jnp.where(live_mask[:, None, :], scores, -1e30)
    row_peak = jnp.max(scores, axis=2)
    weights = jnp.where(live_mask[:, None, :], jnp.exp(scores - row_peak[:, :, None]), 0.0)
    row_total = jnp.sum(weights, axis=2)
    rounded = weights.astype(jnp.bfloat16)
    partial_out = jnp.einsum(
        "rhl,rlc->rhc", rounded, key_rows[:, :, :KVL], preferred_element_type=jnp.float32
    )
    peak_all, total_all, output_all = combined_all(
        (row_peak, row_total, partial_out), "dec", combine_parts
    )
    self_score = (
        jnp.einsum("rhc,rc->rh", dec_query, new_key, preferred_element_type=jnp.float32)
        * softmax_scale
    )
    overall = jnp.maximum(peak_all, self_score)
    carried = jnp.exp(peak_all - overall)
    self_weight = jnp.exp(self_score - overall)
    denom = total_all * carried + self_weight
    numer = output_all * carried[:, :, None] + self_weight[:, :, None] * new_key[
        :, None, :KVL
    ].astype(jnp.float32)
    attn_latent = (numer / denom[:, :, None]).astype(jnp.bfloat16)
    return (q_latent, attn_latent)


def solution(mesh):
    return jax.shard_map(
        body,
        mesh=mesh,
        in_specs=(
            P(("grp", "dec"), ("stg", "tp")),
            P(("stg", "tp"), "dec"),
            P(),
            P(),
            P(("grp", "dec"), None, None),
            P(("grp", "dec"), None),
            P(("grp", "dec"), None, None),
            P("grp", "dec"),
            P("grp", ("stg", "tp"), None),
            P("grp", None),
        ),
        out_specs=(P(("grp", "dec"), ("stg", "tp")), P("grp", ("stg", "tp"), None)),
        check_vma=False,
    )
```

```python
import functools

import jax
import jax.numpy as jnp
from jax import lax
from jax.experimental import pallas as pl
from jax.experimental.pallas import tpu as pltpu
from jax.sharding import PartitionSpec as P

QL = 1536
KVL = 512
ROPE = 64
PAGE = 32


softmax_scale = 192.0 ** (-0.5)
norm_eps = 1e-06


def combined_all(part, axis, combine):
    gathered = jax.tree.map(lambda a: lax.all_gather(a, axis), part)

    def take(source):
        return jax.tree.map(lambda a: lax.dynamic_index_in_dim(a, source, 0, False), gathered)

    return lax.fori_loop(
        1, lax.axis_size(axis), lambda source, state: combine(state, take(source)), take(0)
    )


def rope_rotate(matrix, col_start, positions):
    col_count = matrix.shape[1]
    columns = col_start + jnp.arange(col_count, dtype=jnp.int32)
    is_rope = columns >= KVL
    pair_index = jnp.maximum(columns - KVL, 0) // 2
    frequency = jnp.power(jnp.float32(10000.0), -(2 * pair_index).astype(jnp.float32) / ROPE)
    angles = positions[:, None] * frequency[None, :]
    cosine = jnp.where(is_rope[None, :], jnp.cos(angles), 1.0)
    sine_part = jnp.where(is_rope[None, :], jnp.sin(angles), 0.0)
    paired = matrix.reshape(matrix.shape[0], col_count // 2, 2)
    partner = jnp.stack([-paired[:, :, 1], paired[:, :, 0]], axis=2).reshape(matrix.shape)
    return matrix * cosine + partner * sine_part


def kv_finish(matrix, col_start, latent_sq, kv_gain, positions):
    col_count = matrix.shape[1]
    columns = col_start + jnp.arange(col_count, dtype=jnp.int32)
    gain_full = jnp.concatenate([kv_gain, jnp.ones((ROPE,), jnp.float32)])
    gain_cols = lax.dynamic_slice_in_dim(gain_full, col_start, col_count)
    inverse = lax.rsqrt(latent_sq / KVL + norm_eps)
    row_scale = jnp.where(columns[None, :] < KVL, inverse[:, None] * gain_cols[None, :], 1.0)
    return rope_rotate(matrix * row_scale, col_start, positions).astype(jnp.bfloat16)


def pack_pages(kv_pages, page_table, owner_count, capacity):
    owners = page_table[:, 0]
    slot_ids = page_table[:, 1]
    page_ids = jnp.arange(kv_pages.shape[0], dtype=jnp.int32)
    earlier = (owners[:, None] == owners[None, :]) & (page_ids[None, :] < page_ids[:, None])
    ranking = jnp.sum(earlier.astype(jnp.int32), axis=1)
    targets = owners * capacity + ranking
    places = jnp.arange(owner_count * capacity, dtype=jnp.int32)
    matches = targets[None, :] == places[:, None]
    source_ids = jnp.sum(jnp.where(matches, page_ids[None, :], 0), axis=1)
    filled = jnp.any(matches, axis=1)
    chosen = jnp.where(
        filled[:, None, None], jnp.take(kv_pages, source_ids, axis=0), jnp.zeros((), kv_pages.dtype)
    )
    labels = jnp.where(filled, jnp.take(slot_ids, source_ids), -1).astype(jnp.bfloat16)
    return (
        chosen.reshape(owner_count, capacity, kv_pages.shape[1], kv_pages.shape[2]),
        labels.reshape(owner_count, capacity),
    )


def place_pages(old_cache, got_pages, got_labels):
    flat_pages = got_pages.reshape(-1, old_cache.shape[1], old_cache.shape[2])
    label_ids = got_labels.reshape(-1).astype(jnp.int32)
    slot_ids = jnp.arange(old_cache.shape[0], dtype=jnp.int32)
    arrival_ids = jnp.arange(label_ids.shape[0], dtype=jnp.int32)
    matches = label_ids[None, :] == slot_ids[:, None]
    source_ids = jnp.sum(jnp.where(matches, arrival_ids[None, :], 0), axis=1)
    arrived = jnp.any(matches, axis=1)
    return jnp.where(arrived[:, None, None], jnp.take(flat_pages, source_ids, axis=0), old_cache)


def combine_parts(former, latter):
    overall = jnp.maximum(former[0], latter[0])
    front_scale = jnp.exp(former[0] - overall)
    back_scale = jnp.exp(latter[0] - overall)
    return (
        overall,
        former[1] * front_scale + latter[1] * back_scale,
        former[2] * front_scale[:, :, None] + latter[2] * back_scale[:, :, None],
    )


MESH = pl.DeviceIdType.MESH


def fused_kernel(
    dims, w_ref, x_ref, qg_ref, kg_ref, cos_ref, sin_ref, src_ref, bt_ref, lens_ref,
    plan_ref, want_ref, old_ref, dq_ref, nk_ref, q_out, a_out,
    wbuf, pt, aq, bq, cq, eq, ss, ssin, kvp, bk, ck, ek, kvl, sendp, got, plans,
    found, found_s, kbuf, part, parts, selfs, newk, fin,
    local_sem, zsem, zrecv, ysem, yrecv, t_send, t_recv, s_send, s_recv, v_send, v_recv,
    tk_send, tk_recv, sk_send, sk_recv, l_send, l_recv, pl_send, pl_recv, pg_send, pg_recv,
    c_send, c_recv, f_send, f_recv,
):
    D, G, S, T, K = dims
    C, fg = w_ref.shape[1], w_ref.shape[2]
    qw = qg_ref.shape[0]
    rows, kvw = kvp.shape
    lane_rows = rows // (S * T)
    chunk_rows = C // K
    cap = sendp.shape[1]
    requests, spans = kbuf.shape[0], kbuf.shape[1]
    table_width = spans // PAGE
    fold = part.shape[0] // D
    me, g = lax.axis_index("dec"), lax.axis_index("grp")
    st, tp = lax.axis_index("stg"), lax.axis_index("tp")
    lane = st * T + tp
    lane_steps = [(a, b) for a in range(S) for b in range(T) if a or b]

    def lane_at(a, b):
        return {"stg": lax.rem(st + a, S), "tp": lax.rem(tp + b, T)}

    def remote(src, dst, send, recv, target):
        return pltpu.make_async_remote_copy(
            src_ref=src, dst_ref=dst, send_sem=send, recv_sem=recv,
            device_id=target, device_id_type=MESH,
        )

    own = pltpu.make_async_copy(
        w_ref, wbuf.at[:, pl.ds(pl.multiple_of(me * C, 16), C)], local_sem.at[0]
    )
    own.start()
    barrier = pltpu.get_barrier_semaphore()
    greeted = [{"dec": lax.rem(me + d, D)} for d in range(1, D)]
    greeted += [{"grp": lax.rem(g + d, G)} for d in range(1, G)]
    greeted += [lane_at(a, b) for a, b in lane_steps]
    for target in greeted:
        pl.semaphore_signal(barrier, inc=1, device_id=target, device_id_type=MESH)
    pl.semaphore_wait(barrier, len(greeted))

    def chunk(j, half, c):
        start = pl.multiple_of(j * C + c * chunk_rows, 16)
        return wbuf.at[half, pl.ds(start, chunk_rows)]

    def z_copy(j, c, way, mine):
        src = w_ref.at[g, pl.ds(c * chunk_rows, chunk_rows)] if mine else chunk(j, g, c)
        to = me + 1 if way == 0 else me - 1
        return remote(src, chunk(j, g, c), zsem.at[way, j, c], zrecv.at[j, c], {"dec": to})

    def y_copy(j, c, d):
        return remote(
            chunk(j, g, c), chunk(j, g, c), ysem.at[d - 1, j, c], yrecv.at[d - 1, j, c],
            {"grp": lax.rem(g + d, G)},
        )

    def y_arrive(j, c, d):
        half = lax.rem(g + G - d, G)
        return remote(
            chunk(j, half, c), chunk(j, half, c), ysem.at[d - 1, j, c],
            yrecv.at[d - 1, j, c], {"grp": half},
        )

    def own_left(turn):
        @pl.when((me > 0) & (me == D - 1 - turn))
        def _():
            for c in reversed(range(K)):
                z_copy(me, c, 1, True).start()

    plan_copies = []
    plans[me] = plan_ref[...]
    for d in range(1, D):
        copy = remote(
            plan_ref, plans.at[me], pl_send.at[d - 1], pl_recv.at[d - 1],
            {"dec": lax.rem(me + d, D)},
        )
        copy.start()
        plan_copies.append(copy)
    own_left(0)

    @pl.when(me < D - 1)
    def _():
        for c in reversed(range(K)):
            z_copy(me, c, 0, True).start()

    own.wait()

    def project(j):
        @pl.when(j * C < QL)
        def _():
            block = pl.ds(pl.multiple_of(j * C, 16), C)
            total = None
            for half in range(G):
                term = lax.dot_general(
                    wbuf[half, block, :], x_ref[:, half * fg : (half + 1) * fg],
                    (((1,), (1,)), ((), ())), preferred_element_type=jnp.float32,
                )
                total = term if total is None else total + term
            pt[block, :] = total

    project(me)

    def is_kv(j, c):
        return j * C + (c + 1) * chunk_rows > QL

    def finish_block(j, there):
        for c in range(K):
            @pl.when(there & jnp.logical_not(is_kv(j, c)))
            def _():
                for d in range(1, G):
                    y_arrive(j, c, d).wait_recv()

        @pl.when(there)
        def _():
            project(j)

    def relay(n):
        turn, c = n // K, K - 1 - n % K
        jr, jl = me - 1 - turn, D - 1 - turn
        if n % K == 0 and turn > 0:
            own_left(turn)

        @pl.when(jl > me)
        def _():
            z_copy(jl, c, 1, False).wait_recv()

            @pl.when(me > 0)
            def _():
                z_copy(jl, c, 1, False).start()
            for d in range(1, G):
                y_copy(jl, c, d).start()

        @pl.when(jr >= 0)
        def _():
            z_copy(jr, c, 0, False).wait_recv()

            @pl.when(me < D - 1)
            def _():
                z_copy(jr, c, 0, False).start()

            @pl.when(me == D - 1)
            def _():
                for d in range(1, G):
                    y_copy(jr, c, d).start()
        if turn > 0:
            @pl.when((me < D - 1) & (jr + 1 >= 0))
            def _():
                for d in range(1, G):
                    y_copy(jr + 1, c, d).start()

    tk, sk, lk, pg, cc, ff = [], [], [], [], [], []

    def k_rows(at):
        return kvp.at[pl.ds(pl.multiple_of(at * lane_rows, 16), lane_rows)]

    def kv_project():
        for j in range(D):
            for c in range(K):
                if is_kv(j, c):
                    @pl.when(me != j)
                    def _():
                        for d in range(1, G):
                            y_arrive(j, c, d).wait_recv()
        total = None
        for half in range(G):
            term = lax.dot_general(
                x_ref[:, half * fg : (half + 1) * fg], wbuf[half, QL:, :],
                (((1,), (1,)), ((), ())), preferred_element_type=jnp.float32,
            )
            total = term if total is None else total + term
        kvp[...] = total
        for d in range(1, T):
            t2 = lax.rem(tp + d, T)
            for a in range(S):
                copy = remote(
                    k_rows(a * T + t2), bk.at[d - 1, a], tk_send.at[d - 1, a],
                    tk_recv.at[d - 1, a], {"tp": t2},
                )
                copy.start()
                tk.append(copy)

    def kv_tp(a):
        k = k_rows(a * T + tp)[...]
        for d in range(T - 1):
            k = k + bk[d, a]
        return k

    def kv_across():
        for copy in tk:
            copy.wait_recv()
        for d in range(1, S):
            s2 = lax.rem(st + d, S)
            ck[d - 1] = kv_tp(s2)
            copy = remote(
                ck.at[d - 1], ek.at[d - 1], sk_send.at[d - 1], sk_recv.at[d - 1], {"stg": s2}
            )
            copy.start()
            sk.append(copy)

    def kv_norm():
        for copy in sk:
            copy.wait_recv()
        k = kv_tp(st)
        for d in range(S - 1):
            k = k + ek[d]
        lat, tail = k[:, :KVL], k[:, KVL:]
        square = jnp.sum(lat * lat, axis=1, keepdims=True)
        lat = lat * (lax.rsqrt(square / KVL + norm_eps) * kg_ref[...])
        to = lax.broadcasted_iota(jnp.int32, (ROPE, ROPE), 1)
        at = lax.broadcasted_iota(jnp.int32, (ROPE, ROPE), 0)
        even = lax.rem(to, 2) == 0
        swap = jnp.where(even & (at == to + 1), -1.0, 0.0)
        swap = jnp.where(jnp.logical_not(even) & (at == to - 1), 1.0, swap)
        partner = jnp.dot(
            tail, swap, preferred_element_type=jnp.float32, precision=lax.Precision.HIGHEST
        )
        tail = tail * cos_ref[...] + partner * sin_ref[...]
        pages = lane_rows // PAGE
        mine = pl.ds(lane * pages, pages)
        kvl[mine, :, :KVL] = lat.astype(jnp.bfloat16).reshape(pages, PAGE, KVL)
        kvl[mine, :, KVL:] = tail.astype(jnp.bfloat16).reshape(pages, PAGE, ROPE)
        for i, (a, b) in enumerate(lane_steps):
            copy = remote(
                kvl.at[mine], kvl.at[mine], l_send.at[i], l_recv.at[i], lane_at(a, b)
            )
            copy.start()
            lk.append(copy)
        for copy in plan_copies:
            copy.wait_recv()
        total = jnp.zeros(want_ref.shape, jnp.int32)
        for d in range(D):
            keys, ranks = plans[d, 0:1, :], plans[d, 1:2, :]
            total = total + jnp.where(keys == want_ref[...], d * cap + ranks + 1, 0)
        found[...] = jnp.broadcast_to(jnp.sum(total, axis=1, keepdims=True), found.shape)
        copy = pltpu.make_async_copy(found, found_s, local_sem.at[1])
        copy.start()
        copy.wait()

    def send_pages():
        for copy in lk:
            copy.wait_recv()
        for o in range(D):
            for r in range(cap):
                sendp[o, r] = kvl[src_ref[o * cap + r]]
        for d in range(1, D):
            to = lax.rem(me + d, D)
            copy = remote(
                sendp.at[to], got.at[me], pg_send.at[d - 1], pg_recv.at[d - 1], {"dec": to}
            )
            copy.start()
            pg.append(copy)
        got[me] = sendp[me]
        for r in range(requests):
            query = dq_ref[r].astype(jnp.float32)
            row = nk_ref[pl.ds(r, 1), :].astype(jnp.float32)
            score = jnp.sum(query * row, axis=1, keepdims=True) * softmax_scale
            heads = query.shape[0]
            selfs[r * heads : (r + 1) * heads, :] = jnp.broadcast_to(score, (heads, 128))
            newk[r * heads : (r + 1) * heads, :] = jnp.broadcast_to(row[:, :KVL], (heads, KVL))

    def attend():
        for copy in pg:
            copy.wait_recv()
        for r in range(requests):
            for j in range(table_width):
                place = r * table_width + j
                index = found_s[place, 0]
                came = jnp.clip(index - 1, 0, D * cap - 1)
                fresh = got[came // cap, lax.rem(came, cap)].astype(jnp.float32)
                stale = old_ref[bt_ref[place]].astype(jnp.float32)
                page = jnp.where(jnp.full(fresh.shape, index, jnp.int32) > 0, fresh, stale)
                kbuf[r, j * PAGE : (j + 1) * PAGE, :] = page.astype(jnp.bfloat16)
        for r in range(requests):
            scores = lax.dot_general(
                dq_ref[r], kbuf[r], (((1,), (1,)), ((), ())), preferred_element_type=jnp.float32
            ) * softmax_scale
            live = lax.broadcasted_iota(jnp.int32, scores.shape, 1) < lens_ref[r]
            scores = jnp.where(live, scores, -1e30)
            peak = jnp.max(scores, axis=1, keepdims=True)
            weight = jnp.where(live, jnp.exp(scores - peak), 0.0)
            total = jnp.sum(weight, axis=1, keepdims=True)
            heads = scores.shape[0]
            at = pl.ds(r * heads, heads)
            part[at, :KVL] = jnp.dot(
                weight.astype(jnp.bfloat16), kbuf[r, :, :KVL], preferred_element_type=jnp.float32
            )
            column = lax.broadcasted_iota(jnp.int32, (heads, 128), 1)
            part[at, KVL:] = jnp.where(column < 64, peak, total)
        for d in range(1, D):
            to = lax.rem(me + d, D)
            copy = remote(
                part.at[pl.ds(pl.multiple_of(to * fold, 8), fold)], parts.at[d - 1],
                c_send.at[d - 1], c_recv.at[d - 1], {"dec": to},
            )
            copy.start()
            cc.append(copy)

    def combine():
        for copy in cc:
            copy.wait_recv()
        mine = pl.ds(pl.multiple_of(me * fold, 8), fold)
        shares = [part[mine, :]] + [parts[d] for d in range(D - 1)]
        own_score = selfs[mine, 0:1]
        top = own_score
        for share in shares:
            top = jnp.maximum(top, share[:, KVL : KVL + 1])
        own_weight = jnp.exp(own_score - top)
        numer, denom = own_weight * newk[mine, :], own_weight
        for share in shares:
            factor = jnp.exp(share[:, KVL : KVL + 1] - top)
            numer = numer + factor * share[:, :KVL]
            denom = denom + factor * share[:, KVL + 64 : KVL + 65]
        fin[me] = (numer / denom).astype(jnp.bfloat16)
        for d in range(1, D):
            copy = remote(
                fin.at[me], fin.at[me], f_send.at[d - 1], f_recv.at[d - 1],
                {"dec": lax.rem(me + d, D)},
            )
            copy.start()
            ff.append(copy)

    items = K * (D - 1)
    kv_items = -(-kvw // chunk_rows)
    stages = [kv_project, kv_across, kv_norm, send_pages, attend, combine]
    first = min(kv_items + 3, items - 1)
    gaps = (0, 2, 6, 9, 13, 17)
    due = {}
    for gap, stage in zip(gaps, stages):
        due.setdefault(min(first + gap, items - 1), []).append(stage)
    for n in range(items):
        relay(n)
        if n > first and n % K == (first + 1) % K:
            turn = n // K - 1
            finish_block(me - 1 - turn, (me - 1 - turn >= 0) & (me == D - 1))
            if turn > 0:
                finish_block(me - turn, (me - turn >= 0) & (me < D - 1))
            finish_block(jnp.int32(D - 1 - turn), D - 1 - turn > me)
        for stage in due.get(n, ()):
            stage()
    turn = D - 2
    finish_block(me - 1 - turn, (me - 1 - turn >= 0) & (me == D - 1))
    finish_block(me - turn, (me - turn >= 0) & (me < D - 1))
    finish_block(jnp.int32(D - 1 - turn), D - 1 - turn > me)

    def q_rows(at):
        return pt[pl.ds(pl.multiple_of(at * qw, 16), qw), :]

    near = []
    for a in range(S):
        for d in range(1, T):
            t2 = lax.rem(tp + d, T)
            aq[d - 1, a] = q_rows(a * T + t2).astype(jnp.bfloat16)
            copy = remote(
                aq.at[d - 1, a], bq.at[d - 1, a], t_send.at[d - 1, a], t_recv.at[d - 1, a],
                {"tp": t2},
            )
            copy.start()
            near.append(copy)
    for copy in near:
        copy.wait_recv()

    def q_tp(a):
        q = q_rows(a * T + tp)
        for d in range(T - 1):
            q = q + bq[d, a].astype(jnp.float32)
        return q

    far = []
    for d in range(1, S):
        s2 = lax.rem(st + d, S)
        cq[d - 1] = q_tp(s2).astype(jnp.bfloat16)
        copy = remote(
            cq.at[d - 1], eq.at[d - 1], s_send.at[d - 1], s_recv.at[d - 1], {"stg": s2}
        )
        copy.start()
        far.append(copy)
    q = q_tp(st)
    for copy in ff:
        copy.wait_recv()
    for e in range(D):
        a_out[e * fold : (e + 1) * fold, :] = fin[e]
    for copy in far:
        copy.wait_recv()
    for d in range(S - 1):
        q = q + eq[d].astype(jnp.float32)
    ss[...] = jnp.broadcast_to(jnp.sum(q * q, axis=0, keepdims=True), ss.shape)
    small = []
    for i, (a, b) in enumerate(lane_steps):
        copy = remote(ss, ssin.at[i], v_send.at[i], v_recv.at[i], lane_at(a, b))
        copy.start()
        small.append(copy)
    square = ss[...]
    for i, copy in enumerate(small):
        copy.wait_recv()
        square = square + ssin[i]
    q = q * lax.rsqrt(square[0:1] / QL + norm_eps) * qg_ref[...]
    q_out[...] = jnp.transpose(q).astype(jnp.bfloat16)

    for copy in plan_copies + tk + sk + lk + pg + cc + ff + near + far + small:
        copy.wait_send()
    for c in range(K):
        @pl.when(me > 0)
        def _():
            z_copy(me, c, 1, True).wait_send()

        @pl.when(me < D - 1)
        def _():
            z_copy(me, c, 0, True).wait_send()
        for j in range(D):
            @pl.when((j > me) & (me > 0))
            def _():
                z_copy(j, c, 1, False).wait_send()

            @pl.when((j < me) & (me < D - 1))
            def _():
                z_copy(j, c, 0, False).wait_send()

            @pl.when(j != me)
            def _():
                for d in range(1, G):
                    y_copy(j, c, d).wait_send()


def chunk_count(rows):
    return next((k for k in (11, 3, 2) if rows % (16 * k) == 0), 1)


def fused_ok(hidden_x, proj_weight, dec_query, page_plan):
    D, G, S, T = [lax.axis_size(n) for n in ("dec", "grp", "stg", "tp")]
    lanes, columns = S * T, proj_weight.shape[1]
    return (
        D > 2
        and chunk_count(columns) > 5
        and columns % 16 == 0
        and (D - 2) * columns <= QL
        and hidden_x.shape[0] % 128 == 0
        and hidden_x.shape[0] % (PAGE * lanes) == 0
        and hidden_x.shape[1] % (128 * G) == 0
        and QL % (16 * lanes) == 0
        and dec_query.shape[1] % 16 == 0
        and dec_query.shape[0] * dec_query.shape[1] % (16 * D) == 0
        and page_plan.shape[0] <= 128
    )


def fused(
    hidden_x, proj_weight, q_gain, kv_gain, old_cache, page_plan, block_table, split_lens,
    dec_query, new_key,
):
    D, G, S, T = [lax.axis_size(n) for n in ("dec", "grp", "stg", "tp")]
    L = S * T
    rows, features = hidden_x.shape
    C = proj_weight.shape[1]
    K = chunk_count(C)
    fg, qw, kvw = features // G, QL // L, KVL + ROPE
    lane, me = lax.axis_index(("stg", "tp")), lax.axis_index("dec")
    lane_rows = rows // L
    weight = jnp.transpose(proj_weight.reshape(G, fg, C), (0, 2, 1))
    qg = lax.dynamic_slice_in_dim(q_gain, lane * qw, qw)[:, None]
    positions = (
        me * rows + lane * lane_rows + jnp.arange(lane_rows, dtype=jnp.int32)
    ).astype(jnp.float32)
    pair_index = jnp.arange(ROPE, dtype=jnp.int32) // 2
    frequency = jnp.power(jnp.float32(10000.0), -(2 * pair_index).astype(jnp.float32) / ROPE)
    angles = positions[:, None] * frequency[None, :]
    cosine, sine = jnp.cos(angles), jnp.sin(angles)

    pages, slots = page_plan.shape[0], old_cache.shape[0]
    cap = max(2, -(-pages // D))
    owners = page_plan[:, 0]
    page_ids = jnp.arange(pages, dtype=jnp.int32)
    earlier = (owners[:, None] == owners[None, :]) & (page_ids[None, :] < page_ids[:, None])
    ranking = jnp.sum(earlier.astype(jnp.int32), axis=1)
    places = jnp.arange(D * cap, dtype=jnp.int32)
    matches = (owners * cap + ranking)[None, :] == places[:, None]
    source_ids = jnp.sum(jnp.where(matches, page_ids[None, :], 0), axis=1)
    plan = jnp.stack([owners * slots + page_plan[:, 1], ranking])
    plan = jnp.pad(plan, ((0, 6), (0, 128 - pages)), constant_values=-1)
    table = block_table.reshape(-1)
    want = jnp.broadcast_to((me * slots + table)[:, None], (table.shape[0], 128))
    requests, heads = dec_query.shape[0], dec_query.shape[1]
    width = block_table.shape[2]
    fold = requests * heads // D
    dma = pltpu.SemaphoreType.DMA
    bf, f32, i32 = jnp.bfloat16, jnp.float32, jnp.int32
    t1, s1, g1, l1, d1 = max(T - 1, 1), max(S - 1, 1), max(G - 1, 1), max(L - 1, 1), D - 1
    vmem = pl.BlockSpec(memory_space=pltpu.VMEM)
    smem = pl.BlockSpec(memory_space=pltpu.SMEM)
    q_out, a_out = pl.pallas_call(
        functools.partial(fused_kernel, (D, G, S, T, K)),
        out_shape=(
            jax.ShapeDtypeStruct((rows, qw), bf),
            jax.ShapeDtypeStruct((requests * heads, KVL), bf),
        ),
        in_specs=[vmem] * 6 + [smem] * 3 + [vmem] * 5,
        out_specs=(vmem, vmem),
        scratch_shapes=[
            pltpu.VMEM((G, D * C, fg), bf),
            pltpu.VMEM((D * C, rows), f32),
            pltpu.VMEM((t1, S, qw, rows), bf),
            pltpu.VMEM((t1, S, qw, rows), bf),
            pltpu.VMEM((s1, qw, rows), bf),
            pltpu.VMEM((s1, qw, rows), bf),
            pltpu.VMEM((8, rows), f32),
            pltpu.VMEM((l1, 8, rows), f32),
            pltpu.VMEM((rows, kvw), f32),
            pltpu.VMEM((t1, S, lane_rows, kvw), f32),
            pltpu.VMEM((s1, lane_rows, kvw), f32),
            pltpu.VMEM((s1, lane_rows, kvw), f32),
            pltpu.VMEM((pages, PAGE, kvw), bf),
            pltpu.VMEM((D, cap, PAGE, kvw), bf),
            pltpu.VMEM((D, cap, PAGE, kvw), bf),
            pltpu.VMEM((D, 8, 128), i32),
            pltpu.VMEM((table.shape[0], 128), i32),
            pltpu.SMEM((table.shape[0], 128), i32),
            pltpu.VMEM((requests, width * PAGE, kvw), bf),
            pltpu.VMEM((requests * heads, KVL + 128), f32),
            pltpu.VMEM((d1, fold, KVL + 128), f32),
            pltpu.VMEM((requests * heads, 128), f32),
            pltpu.VMEM((requests * heads, KVL), f32),
            pltpu.VMEM((D, fold, KVL), bf),
            dma((2,)), dma((2, D, K)), dma((D, K)), dma((g1, D, K)), dma((g1, D, K)),
            dma((t1, S)), dma((t1, S)), dma((s1,)), dma((s1,)), dma((l1,)), dma((l1,)),
            dma((t1, S)), dma((t1, S)), dma((s1,)), dma((s1,)), dma((l1,)), dma((l1,)),
            dma((d1,)), dma((d1,)), dma((d1,)), dma((d1,)),
            dma((d1,)), dma((d1,)), dma((d1,)), dma((d1,)),
        ],
        compiler_params=pltpu.CompilerParams(
            collective_id=0, has_side_effects=True, vmem_limit_bytes=56 * 1024 * 1024
        ),
    )(
        weight, hidden_x, qg, kv_gain[None, :], cosine, sine, source_ids, table,
        split_lens[:, 0], plan, want, old_cache, dec_query, new_key,
    )
    return q_out, a_out.reshape(requests, heads, KVL)


def body(
    hidden_x,
    proj_weight,
    q_gain,
    kv_gain,
    old_cache,
    page_plan,
    block_table,
    split_lens,
    dec_query,
    new_key,
):
    if fused_ok(hidden_x, proj_weight, dec_query, page_plan):
        return fused(
            hidden_x, proj_weight, q_gain, kv_gain, old_cache, page_plan, block_table,
            split_lens, dec_query, new_key,
        )
    projected = jnp.dot(
        hidden_x,
        lax.all_gather(proj_weight, "dec", axis=1, tiled=True),
        preferred_element_type=jnp.float32,
    )
    query_part = projected[:, :QL]
    kv_part = projected[:, QL:]
    tokens_here = hidden_x.shape[0]
    positions = (
        lax.axis_index("dec") * tokens_here + jnp.arange(tokens_here, dtype=jnp.int32)
    ).astype(jnp.float32)
    lane_count = lax.axis_size(("stg", "tp"))
    lane_index = lax.axis_index(("stg", "tp"))
    owner_count = lax.axis_size("dec")
    page_count = page_plan.shape[0]
    capacity = max(2, -(-page_count // owner_count))
    query_width = QL // lane_count
    query_cols, kv_cols = (
        lax.psum_scatter(query_part, ("stg", "tp"), scatter_dimension=1, tiled=True),
        lax.psum_scatter(kv_part, ("stg", "tp"), scatter_dimension=1, tiled=True),
    )
    kv_width = kv_cols.shape[1]
    col_start = lane_index * kv_width
    columns = col_start + jnp.arange(kv_width, dtype=jnp.int32)
    latent_part_sq = jnp.sum(jnp.where(columns[None, :] < KVL, kv_cols * kv_cols, 0.0), axis=1)
    query_sq, latent_sq = lax.psum(
        (jnp.sum(query_cols * query_cols, axis=1), latent_part_sq), ("stg", "tp")
    )
    kv_rows = kv_finish(kv_cols, col_start, latent_sq, kv_gain, positions)
    kv_pages = kv_rows.reshape(page_count, PAGE, kv_width)
    send_pages, send_labels = pack_pages(kv_pages, page_plan, owner_count, capacity)
    got_slices, got_labels = (
        lax.all_to_all(send_pages, "dec", split_axis=0, concat_axis=0, tiled=True),
        lax.all_to_all(send_labels, "dec", split_axis=0, concat_axis=0, tiled=True),
    )
    got_pages = lax.all_gather(got_slices, ("stg", "tp"), axis=3, tiled=True)
    query_gain = lax.dynamic_slice_in_dim(q_gain, lane_index * query_width, query_width)
    q_latent = (
        query_cols * lax.rsqrt(query_sq / QL + norm_eps)[:, None] * query_gain[None, :]
    ).astype(jnp.bfloat16)
    cache = place_pages(old_cache, got_pages, got_labels)
    slot_table = block_table[0]
    request_count = slot_table.shape[0]
    key_rows = jnp.take(cache, slot_table.reshape(-1), axis=0).reshape(
        request_count, -1, cache.shape[2]
    )
    scores = (
        jnp.einsum("rhc,rlc->rhl", dec_query, key_rows, preferred_element_type=jnp.float32)
        * softmax_scale
    )
    live_mask = jnp.arange(key_rows.shape[1], dtype=jnp.int32)[None, :] < split_lens[:, 0][:, None]
    scores = jnp.where(live_mask[:, None, :], scores, -1e30)
    row_peak = jnp.max(scores, axis=2)
    weights = jnp.where(live_mask[:, None, :], jnp.exp(scores - row_peak[:, :, None]), 0.0)
    row_total = jnp.sum(weights, axis=2)
    rounded = weights.astype(jnp.bfloat16)
    partial_out = jnp.einsum(
        "rhl,rlc->rhc", rounded, key_rows[:, :, :KVL], preferred_element_type=jnp.float32
    )
    peak_all, total_all, output_all = combined_all(
        (row_peak, row_total, partial_out), "dec", combine_parts
    )
    self_score = (
        jnp.einsum("rhc,rc->rh", dec_query, new_key, preferred_element_type=jnp.float32)
        * softmax_scale
    )
    overall = jnp.maximum(peak_all, self_score)
    carried = jnp.exp(peak_all - overall)
    self_weight = jnp.exp(self_score - overall)
    denom = total_all * carried + self_weight
    numer = output_all * carried[:, :, None] + self_weight[:, :, None] * new_key[
        :, None, :KVL
    ].astype(jnp.float32)
    attn_latent = (numer / denom[:, :, None]).astype(jnp.bfloat16)
    return (q_latent, attn_latent)


def solution(mesh):
    return jax.shard_map(
        body,
        mesh=mesh,
        in_specs=(
            P(("grp", "dec"), ("stg", "tp")),
            P(("stg", "tp"), "dec"),
            P(),
            P(),
            P(("grp", "dec"), None, None),
            P(("grp", "dec"), None),
            P(("grp", "dec"), None, None),
            P("grp", "dec"),
            P("grp", ("stg", "tp"), None),
            P("grp", None),
        ),
        out_specs=(P(("grp", "dec"), ("stg", "tp")), P("grp", ("stg", "tp"), None)),
        check_vma=False,
    )
```

```python
import functools

import jax
import jax.numpy as jnp
from jax import lax
from jax.experimental import pallas as pl
from jax.experimental.pallas import tpu as pltpu
from jax.sharding import PartitionSpec as P

QL = 1536
KVL = 512
ROPE = 64
PAGE = 32


softmax_scale = 192.0 ** (-0.5)
norm_eps = 1e-06


def combined_all(part, axis, combine):
    gathered = jax.tree.map(lambda a: lax.all_gather(a, axis), part)

    def take(source):
        return jax.tree.map(lambda a: lax.dynamic_index_in_dim(a, source, 0, False), gathered)

    return lax.fori_loop(
        1, lax.axis_size(axis), lambda source, state: combine(state, take(source)), take(0)
    )


def rope_rotate(matrix, col_start, positions):
    col_count = matrix.shape[1]
    columns = col_start + jnp.arange(col_count, dtype=jnp.int32)
    is_rope = columns >= KVL
    pair_index = jnp.maximum(columns - KVL, 0) // 2
    frequency = jnp.power(jnp.float32(10000.0), -(2 * pair_index).astype(jnp.float32) / ROPE)
    angles = positions[:, None] * frequency[None, :]
    cosine = jnp.where(is_rope[None, :], jnp.cos(angles), 1.0)
    sine_part = jnp.where(is_rope[None, :], jnp.sin(angles), 0.0)
    paired = matrix.reshape(matrix.shape[0], col_count // 2, 2)
    partner = jnp.stack([-paired[:, :, 1], paired[:, :, 0]], axis=2).reshape(matrix.shape)
    return matrix * cosine + partner * sine_part


def kv_finish(matrix, col_start, latent_sq, kv_gain, positions):
    col_count = matrix.shape[1]
    columns = col_start + jnp.arange(col_count, dtype=jnp.int32)
    gain_full = jnp.concatenate([kv_gain, jnp.ones((ROPE,), jnp.float32)])
    gain_cols = lax.dynamic_slice_in_dim(gain_full, col_start, col_count)
    inverse = lax.rsqrt(latent_sq / KVL + norm_eps)
    row_scale = jnp.where(columns[None, :] < KVL, inverse[:, None] * gain_cols[None, :], 1.0)
    return rope_rotate(matrix * row_scale, col_start, positions).astype(jnp.bfloat16)


def pack_pages(kv_pages, page_table, owner_count, capacity):
    owners = page_table[:, 0]
    slot_ids = page_table[:, 1]
    page_ids = jnp.arange(kv_pages.shape[0], dtype=jnp.int32)
    earlier = (owners[:, None] == owners[None, :]) & (page_ids[None, :] < page_ids[:, None])
    ranking = jnp.sum(earlier.astype(jnp.int32), axis=1)
    targets = owners * capacity + ranking
    places = jnp.arange(owner_count * capacity, dtype=jnp.int32)
    matches = targets[None, :] == places[:, None]
    source_ids = jnp.sum(jnp.where(matches, page_ids[None, :], 0), axis=1)
    filled = jnp.any(matches, axis=1)
    chosen = jnp.where(
        filled[:, None, None], jnp.take(kv_pages, source_ids, axis=0), jnp.zeros((), kv_pages.dtype)
    )
    labels = jnp.where(filled, jnp.take(slot_ids, source_ids), -1).astype(jnp.bfloat16)
    return (
        chosen.reshape(owner_count, capacity, kv_pages.shape[1], kv_pages.shape[2]),
        labels.reshape(owner_count, capacity),
    )


def place_pages(old_cache, got_pages, got_labels):
    flat_pages = got_pages.reshape(-1, old_cache.shape[1], old_cache.shape[2])
    label_ids = got_labels.reshape(-1).astype(jnp.int32)
    slot_ids = jnp.arange(old_cache.shape[0], dtype=jnp.int32)
    arrival_ids = jnp.arange(label_ids.shape[0], dtype=jnp.int32)
    matches = label_ids[None, :] == slot_ids[:, None]
    source_ids = jnp.sum(jnp.where(matches, arrival_ids[None, :], 0), axis=1)
    arrived = jnp.any(matches, axis=1)
    return jnp.where(arrived[:, None, None], jnp.take(flat_pages, source_ids, axis=0), old_cache)


def combine_parts(former, latter):
    overall = jnp.maximum(former[0], latter[0])
    front_scale = jnp.exp(former[0] - overall)
    back_scale = jnp.exp(latter[0] - overall)
    return (
        overall,
        former[1] * front_scale + latter[1] * back_scale,
        former[2] * front_scale[:, :, None] + latter[2] * back_scale[:, :, None],
    )


MESH = pl.DeviceIdType.MESH


def fused_kernel(
    dims, w_ref, x_ref, qg_ref, kg_ref, cos_ref, sin_ref, src_ref, bt_ref, lens_ref,
    plan_ref, want_ref, old_ref, dq_ref, nk_ref, q_out, a_out,
    wbuf, pt, aq, bq, cq, eq, ss, ssin, kvp, bk, ck, ek, kvl, sendp, got, plans,
    found, found_s, kbuf, part, parts, selfs, newk, fin,
    local_sem, zsem, zrecv, ysem, yrecv, t_send, t_recv, s_send, s_recv, v_send, v_recv,
    tk_send, tk_recv, sk_send, sk_recv, l_send, l_recv, pl_send, pl_recv, pg_send, pg_recv,
    c_send, c_recv, f_send, f_recv,
):
    D, G, S, T, K = dims
    C, fg = w_ref.shape[1], w_ref.shape[2]
    qw = q_out.shape[1]
    rows, kvw = kvp.shape
    lane_rows = rows // (S * T)
    chunk_rows = C // K
    cap = sendp.shape[1]
    requests, spans = kbuf.shape[0], kbuf.shape[1]
    table_width = spans // PAGE
    fold = part.shape[0] // D
    me, g = lax.axis_index("dec"), lax.axis_index("grp")
    st, tp = lax.axis_index("stg"), lax.axis_index("tp")
    lane = st * T + tp
    lane_steps = [(a, b) for a in range(S) for b in range(T) if a or b]

    def lane_at(a, b):
        return {"stg": lax.rem(st + a, S), "tp": lax.rem(tp + b, T)}

    def remote(src, dst, send, recv, target):
        return pltpu.make_async_remote_copy(
            src_ref=src, dst_ref=dst, send_sem=send, recv_sem=recv,
            device_id=target, device_id_type=MESH,
        )

    own = pltpu.make_async_copy(
        w_ref, wbuf.at[:, pl.ds(pl.multiple_of(me * C, 16), C)], local_sem.at[0]
    )
    own.start()
    barrier = pltpu.get_barrier_semaphore()
    greeted = [{"dec": lax.rem(me + d, D)} for d in range(1, D)]
    greeted += [{"grp": lax.rem(g + d, G)} for d in range(1, G)]
    greeted += [lane_at(a, b) for a, b in lane_steps]
    for target in greeted:
        pl.semaphore_signal(barrier, inc=1, device_id=target, device_id_type=MESH)
    pl.semaphore_wait(barrier, len(greeted))

    def chunk(j, half, c):
        start = pl.multiple_of(j * C + c * chunk_rows, 16)
        return wbuf.at[half, pl.ds(start, chunk_rows)]

    def z_copy(j, c, way, mine):
        src = w_ref.at[g, pl.ds(c * chunk_rows, chunk_rows)] if mine else chunk(j, g, c)
        to = me + 1 if way == 0 else me - 1
        return remote(src, chunk(j, g, c), zsem.at[way, j, c], zrecv.at[j, c], {"dec": to})

    def y_copy(j, c, d):
        return remote(
            chunk(j, g, c), chunk(j, g, c), ysem.at[d - 1, j, c], yrecv.at[d - 1, j, c],
            {"grp": lax.rem(g + d, G)},
        )

    def y_arrive(j, c, d):
        half = lax.rem(g + G - d, G)
        return remote(
            chunk(j, half, c), chunk(j, half, c), ysem.at[d - 1, j, c],
            yrecv.at[d - 1, j, c], {"grp": half},
        )

    def own_left(turn, c):
        @pl.when((me > 0) & (me == D - 1 - turn))
        def _():
            if turn > 0 and c < K - 2:
                z_copy(me, c + 2, 1, True).wait_send()
            z_copy(me, c, 1, True).start()

    plan_copies = []
    plans[me] = plan_ref[...]
    for d in range(1, D):
        copy = remote(
            plan_ref, plans.at[me], pl_send.at[d - 1], pl_recv.at[d - 1],
            {"dec": lax.rem(me + d, D)},
        )
        copy.start()
        plan_copies.append(copy)
    for c in reversed(range(K)):
        own_left(0, c)

    @pl.when(me < D - 1)
    def _():
        for c in reversed(range(K)):
            z_copy(me, c, 0, True).start()

    own.wait()

    def project(j):
        @pl.when(j * C < QL)
        def _():
            block = pl.ds(pl.multiple_of(j * C, 16), C)
            total = None
            for half in range(G):
                term = lax.dot_general(
                    wbuf[half, block, :], x_ref[:, half * fg : (half + 1) * fg],
                    (((1,), (1,)), ((), ())), preferred_element_type=jnp.float32,
                )
                total = term if total is None else total + term
            pt[block, :] = total

    project(me)

    def is_kv(j, c):
        return j * C + (c + 1) * chunk_rows > QL

    def finish_block(j, there):
        for c in range(K):
            @pl.when(there & jnp.logical_not(is_kv(j, c)))
            def _():
                for d in range(1, G):
                    y_arrive(j, c, d).wait_recv()

        @pl.when(there)
        def _():
            project(j)

    def relay(n):
        turn, c = n // K, K - 1 - n % K
        jr, jl = me - 1 - turn, D - 1 - turn
        if turn > 0:
            own_left(turn, c)

        @pl.when(jl > me)
        def _():
            z_copy(jl, c, 1, False).wait_recv()

            @pl.when(me > 0)
            def _():
                z_copy(jl, c, 1, False).start()
            for d in range(1, G):
                y_copy(jl, c, d).start()

        @pl.when(jr >= 0)
        def _():
            z_copy(jr, c, 0, False).wait_recv()

            @pl.when(me < D - 1)
            def _():
                z_copy(jr, c, 0, False).start()

            @pl.when(me == D - 1)
            def _():
                for d in range(1, G):
                    y_copy(jr, c, d).start()
        if turn > 0:
            @pl.when((me < D - 1) & (jr + 1 >= 0))
            def _():
                for d in range(1, G):
                    y_copy(jr + 1, c, d).start()

    tk, sk, lk, pg, cc, ff = [], [], [], [], [], []

    def k_rows(at):
        return kvp.at[pl.ds(pl.multiple_of(at * lane_rows, 16), lane_rows)]

    def kv_project():
        for j in range(D):
            for c in range(K):
                if is_kv(j, c):
                    @pl.when(me != j)
                    def _():
                        for d in range(1, G):
                            y_arrive(j, c, d).wait_recv()
        total = None
        for half in range(G):
            term = lax.dot_general(
                x_ref[:, half * fg : (half + 1) * fg], wbuf[half, QL:, :],
                (((1,), (1,)), ((), ())), preferred_element_type=jnp.float32,
            )
            total = term if total is None else total + term
        kvp[...] = total
        for d in range(1, T):
            t2 = lax.rem(tp + d, T)
            for a in range(S):
                copy = remote(
                    k_rows(a * T + t2), bk.at[d - 1, a], tk_send.at[d - 1, a],
                    tk_recv.at[d - 1, a], {"tp": t2},
                )
                copy.start()
                tk.append(copy)

    def kv_tp(a):
        k = k_rows(a * T + tp)[...]
        for d in range(T - 1):
            k = k + bk[d, a]
        return k

    def kv_across():
        for copy in tk:
            copy.wait_recv()
        for d in range(1, S):
            s2 = lax.rem(st + d, S)
            ck[d - 1] = kv_tp(s2)
            copy = remote(
                ck.at[d - 1], ek.at[d - 1], sk_send.at[d - 1], sk_recv.at[d - 1], {"stg": s2}
            )
            copy.start()
            sk.append(copy)

    def kv_norm():
        for copy in sk:
            copy.wait_recv()
        k = kv_tp(st)
        for d in range(S - 1):
            k = k + ek[d]
        lat, tail = k[:, :KVL], k[:, KVL:]
        square = jnp.sum(lat * lat, axis=1, keepdims=True)
        lat = lat * (lax.rsqrt(square / KVL + norm_eps) * kg_ref[...])
        to = lax.broadcasted_iota(jnp.int32, (ROPE, ROPE), 1)
        at = lax.broadcasted_iota(jnp.int32, (ROPE, ROPE), 0)
        even = lax.rem(to, 2) == 0
        swap = jnp.where(even & (at == to + 1), -1.0, 0.0)
        swap = jnp.where(jnp.logical_not(even) & (at == to - 1), 1.0, swap)
        partner = jnp.dot(
            tail, swap, preferred_element_type=jnp.float32, precision=lax.Precision.HIGHEST
        )
        tail = tail * cos_ref[...] + partner * sin_ref[...]
        pages = lane_rows // PAGE
        mine = pl.ds(lane * pages, pages)
        kvl[mine, :, :KVL] = lat.astype(jnp.bfloat16).reshape(pages, PAGE, KVL)
        kvl[mine, :, KVL:] = tail.astype(jnp.bfloat16).reshape(pages, PAGE, ROPE)
        for i, (a, b) in enumerate(lane_steps):
            copy = remote(
                kvl.at[mine], kvl.at[mine], l_send.at[i], l_recv.at[i], lane_at(a, b)
            )
            copy.start()
            lk.append(copy)
        for copy in plan_copies:
            copy.wait_recv()
        total = jnp.zeros(want_ref.shape, jnp.int32)
        for d in range(D):
            keys, ranks = plans[d, 0:1, :], plans[d, 1:2, :]
            total = total + jnp.where(keys == want_ref[...], d * cap + ranks + 1, 0)
        found[...] = jnp.broadcast_to(jnp.sum(total, axis=1, keepdims=True), found.shape)
        copy = pltpu.make_async_copy(found, found_s, local_sem.at[1])
        copy.start()
        copy.wait()

    def send_pages():
        for copy in lk:
            copy.wait_recv()
        for o in range(D):
            for r in range(cap):
                sendp[o, r] = kvl[src_ref[o * cap + r]]
        for d in range(1, D):
            to = lax.rem(me + d, D)
            copy = remote(
                sendp.at[to], got.at[me], pg_send.at[d - 1], pg_recv.at[d - 1], {"dec": to}
            )
            copy.start()
            pg.append(copy)
        got[me] = sendp[me]
        for r in range(requests):
            query = dq_ref[r].astype(jnp.float32)
            row = nk_ref[pl.ds(r, 1), :].astype(jnp.float32)
            score = jnp.sum(query * row, axis=1, keepdims=True) * softmax_scale
            heads = query.shape[0]
            selfs[r * heads : (r + 1) * heads, :] = jnp.broadcast_to(score, (heads, 128))
            newk[r * heads : (r + 1) * heads, :] = jnp.broadcast_to(row[:, :KVL], (heads, KVL))

    def attend():
        for copy in pg:
            copy.wait_recv()
        for r in range(requests):
            for j in range(table_width):
                place = r * table_width + j
                index = found_s[place, 0]
                came = jnp.clip(index - 1, 0, D * cap - 1)
                fresh = got[came // cap, lax.rem(came, cap)].astype(jnp.float32)
                stale = old_ref[bt_ref[place]].astype(jnp.float32)
                page = jnp.where(jnp.full(fresh.shape, index, jnp.int32) > 0, fresh, stale)
                kbuf[r, j * PAGE : (j + 1) * PAGE, :] = page.astype(jnp.bfloat16)
        for r in range(requests):
            scores = lax.dot_general(
                dq_ref[r], kbuf[r], (((1,), (1,)), ((), ())), preferred_element_type=jnp.float32
            ) * softmax_scale
            live = lax.broadcasted_iota(jnp.int32, scores.shape, 1) < lens_ref[r]
            scores = jnp.where(live, scores, -1e30)
            peak = jnp.max(scores, axis=1, keepdims=True)
            weight = jnp.where(live, jnp.exp(scores - peak), 0.0)
            total = jnp.sum(weight, axis=1, keepdims=True)
            heads = scores.shape[0]
            at = pl.ds(r * heads, heads)
            part[at, :KVL] = jnp.dot(
                weight.astype(jnp.bfloat16), kbuf[r, :, :KVL], preferred_element_type=jnp.float32
            )
            column = lax.broadcasted_iota(jnp.int32, (heads, 128), 1)
            part[at, KVL:] = jnp.where(column < 64, peak, total)
        for d in range(1, D):
            to = lax.rem(me + d, D)
            copy = remote(
                part.at[pl.ds(pl.multiple_of(to * fold, 8), fold)], parts.at[d - 1],
                c_send.at[d - 1], c_recv.at[d - 1], {"dec": to},
            )
            copy.start()
            cc.append(copy)

    def combine():
        for copy in cc:
            copy.wait_recv()
        mine = pl.ds(pl.multiple_of(me * fold, 8), fold)
        shares = [part[mine, :]] + [parts[d] for d in range(D - 1)]
        own_score = selfs[mine, 0:1]
        top = own_score
        for share in shares:
            top = jnp.maximum(top, share[:, KVL : KVL + 1])
        own_weight = jnp.exp(own_score - top)
        numer, denom = own_weight * newk[mine, :], own_weight
        for share in shares:
            factor = jnp.exp(share[:, KVL : KVL + 1] - top)
            numer = numer + factor * share[:, :KVL]
            denom = denom + factor * share[:, KVL + 64 : KVL + 65]
        fin[me] = (numer / denom).astype(jnp.bfloat16)
        for d in range(1, D):
            copy = remote(
                fin.at[me], fin.at[me], f_send.at[d - 1], f_recv.at[d - 1],
                {"dec": lax.rem(me + d, D)},
            )
            copy.start()
            ff.append(copy)

    items = K * (D - 1)
    kv_items = -(-kvw // chunk_rows)
    stages = [kv_project, kv_across, kv_norm, send_pages, attend, combine]
    first = min(kv_items + 3, items - 1)
    gaps = (0, 2, 6, 9, 13, 17)
    due = {}
    for gap, stage in zip(gaps, stages):
        due.setdefault(min(first + gap, items - 1), []).append(stage)
    for n in range(items):
        relay(n)
        if n > first and n % K == (first + 1) % K:
            turn = n // K - 1
            finish_block(me - 1 - turn, (me - 1 - turn >= 0) & (me == D - 1))
            if turn > 0:
                finish_block(me - turn, (me - turn >= 0) & (me < D - 1))
            finish_block(jnp.int32(D - 1 - turn), D - 1 - turn > me)
        for stage in due.get(n, ()):
            stage()
    turn = D - 2
    finish_block(me - 1 - turn, (me - 1 - turn >= 0) & (me == D - 1))
    finish_block(me - turn, (me - turn >= 0) & (me < D - 1))
    finish_block(jnp.int32(D - 1 - turn), D - 1 - turn > me)

    def q_rows(at):
        return pt[pl.ds(pl.multiple_of(at * qw, 16), qw), :]

    near = []
    for i in range(1, S + 1):
        a = lax.rem(st + i, S)
        group = []
        for d in range(1, T):
            t2 = lax.rem(tp + d, T)
            aq[d - 1, a] = q_rows(a * T + t2).astype(jnp.bfloat16)
            copy = remote(
                aq.at[d - 1, a], bq.at[d - 1, a], t_send.at[d - 1, a], t_recv.at[d - 1, a],
                {"tp": t2},
            )
            copy.start()
            group.append(copy)
        near.append(group)

    def q_tp(a):
        q = q_rows(a * T + tp)
        for d in range(T - 1):
            q = q + bq[d, a].astype(jnp.float32)
        return q

    far = []
    for d in range(1, S):
        s2 = lax.rem(st + d, S)
        for copy in near[d - 1]:
            copy.wait_recv()
        cq[d - 1] = q_tp(s2).astype(jnp.bfloat16)
        copy = remote(
            cq.at[d - 1], eq.at[d - 1], s_send.at[d - 1], s_recv.at[d - 1], {"stg": s2}
        )
        copy.start()
        far.append(copy)
    for copy in near[S - 1]:
        copy.wait_recv()
    q = q_tp(st)
    for copy in ff:
        copy.wait_recv()
    for e in range(D):
        a_out[e * fold : (e + 1) * fold, :] = fin[e]
    for copy in far:
        copy.wait_recv()
    for d in range(S - 1):
        q = q + eq[d].astype(jnp.float32)
    ss[...] = jnp.broadcast_to(jnp.sum(q * q, axis=0, keepdims=True), ss.shape)
    small = []
    for i, (a, b) in enumerate(lane_steps):
        copy = remote(ss, ssin.at[i], v_send.at[i], v_recv.at[i], lane_at(a, b))
        copy.start()
        small.append(copy)
    square = ss[...]
    for i, copy in enumerate(small):
        copy.wait_recv()
        square = square + ssin[i]
    q = jnp.transpose(q * lax.rsqrt(square[0:1] / QL + norm_eps))
    gain = qg_ref[:, pl.ds(pl.multiple_of(lane * qw, 128), qw)]
    q_out[...] = (q * gain).astype(jnp.bfloat16)

    for copy in plan_copies + tk + sk + lk + pg + cc + ff + sum(near, []) + far + small:
        copy.wait_send()
    for c in range(K):
        @pl.when((me > 0) if c < 2 else (me == D - 1))
        def _():
            z_copy(me, c, 1, True).wait_send()

        @pl.when(me < D - 1)
        def _():
            z_copy(me, c, 0, True).wait_send()
        for j in range(D):
            @pl.when((j > me) & (me > 0))
            def _():
                z_copy(j, c, 1, False).wait_send()

            @pl.when((j < me) & (me < D - 1))
            def _():
                z_copy(j, c, 0, False).wait_send()

            @pl.when(j != me)
            def _():
                for d in range(1, G):
                    y_copy(j, c, d).wait_send()


def chunk_count(rows):
    return next((k for k in (11, 3, 2) if rows % (16 * k) == 0), 1)


def fused_ok(hidden_x, proj_weight, dec_query, page_plan):
    D, G, S, T = [lax.axis_size(n) for n in ("dec", "grp", "stg", "tp")]
    lanes, columns = S * T, proj_weight.shape[1]
    return (
        D > 2
        and chunk_count(columns) > 5
        and columns % 16 == 0
        and (D - 2) * columns <= QL
        and hidden_x.shape[0] % 128 == 0
        and hidden_x.shape[0] % (PAGE * lanes) == 0
        and hidden_x.shape[1] % (128 * G) == 0
        and QL % (128 * lanes) == 0
        and dec_query.shape[1] % 16 == 0
        and dec_query.shape[0] * dec_query.shape[1] % (16 * D) == 0
        and page_plan.shape[0] <= 128
    )


def fused(
    hidden_x, proj_weight, q_gain, kv_gain, old_cache, page_plan, block_table, split_lens,
    dec_query, new_key,
):
    D, G, S, T = [lax.axis_size(n) for n in ("dec", "grp", "stg", "tp")]
    L = S * T
    rows, features = hidden_x.shape
    C = proj_weight.shape[1]
    K = chunk_count(C)
    fg, qw, kvw = features // G, QL // L, KVL + ROPE
    lane, me = lax.axis_index(("stg", "tp")), lax.axis_index("dec")
    lane_rows = rows // L
    weight = jnp.transpose(proj_weight.reshape(G, fg, C), (0, 2, 1))
    qg = q_gain[None, :]
    positions = (
        me * rows + lane * lane_rows + jnp.arange(lane_rows, dtype=jnp.int32)
    ).astype(jnp.float32)
    pair_index = jnp.arange(ROPE, dtype=jnp.int32) // 2
    frequency = jnp.power(jnp.float32(10000.0), -(2 * pair_index).astype(jnp.float32) / ROPE)
    angles = positions[:, None] * frequency[None, :]
    cosine, sine = jnp.cos(angles), jnp.sin(angles)

    pages, slots = page_plan.shape[0], old_cache.shape[0]
    cap = max(2, -(-pages // D))
    owners = page_plan[:, 0]
    page_ids = jnp.arange(pages, dtype=jnp.int32)
    earlier = (owners[:, None] == owners[None, :]) & (page_ids[None, :] < page_ids[:, None])
    ranking = jnp.sum(earlier.astype(jnp.int32), axis=1)
    places = jnp.arange(D * cap, dtype=jnp.int32)
    matches = (owners * cap + ranking)[None, :] == places[:, None]
    source_ids = jnp.sum(jnp.where(matches, page_ids[None, :], 0), axis=1)
    plan = jnp.stack([owners * slots + page_plan[:, 1], ranking])
    plan = jnp.pad(plan, ((0, 6), (0, 128 - pages)), constant_values=-1)
    table = block_table.reshape(-1)
    want = jnp.broadcast_to((me * slots + table)[:, None], (table.shape[0], 128))
    requests, heads = dec_query.shape[0], dec_query.shape[1]
    width = block_table.shape[2]
    fold = requests * heads // D
    dma = pltpu.SemaphoreType.DMA
    bf, f32, i32 = jnp.bfloat16, jnp.float32, jnp.int32
    t1, s1, g1, l1, d1 = max(T - 1, 1), max(S - 1, 1), max(G - 1, 1), max(L - 1, 1), D - 1
    vmem = pl.BlockSpec(memory_space=pltpu.VMEM)
    smem = pl.BlockSpec(memory_space=pltpu.SMEM)
    q_out, a_out = pl.pallas_call(
        functools.partial(fused_kernel, (D, G, S, T, K)),
        out_shape=(
            jax.ShapeDtypeStruct((rows, qw), bf),
            jax.ShapeDtypeStruct((requests * heads, KVL), bf),
        ),
        in_specs=[vmem] * 6 + [smem] * 3 + [vmem] * 5,
        out_specs=(vmem, vmem),
        scratch_shapes=[
            pltpu.VMEM((G, D * C, fg), bf),
            pltpu.VMEM((D * C, rows), f32),
            pltpu.VMEM((t1, S, qw, rows), bf),
            pltpu.VMEM((t1, S, qw, rows), bf),
            pltpu.VMEM((s1, qw, rows), bf),
            pltpu.VMEM((s1, qw, rows), bf),
            pltpu.VMEM((8, rows), f32),
            pltpu.VMEM((l1, 8, rows), f32),
            pltpu.VMEM((rows, kvw), f32),
            pltpu.VMEM((t1, S, lane_rows, kvw), f32),
            pltpu.VMEM((s1, lane_rows, kvw), f32),
            pltpu.VMEM((s1, lane_rows, kvw), f32),
            pltpu.VMEM((pages, PAGE, kvw), bf),
            pltpu.VMEM((D, cap, PAGE, kvw), bf),
            pltpu.VMEM((D, cap, PAGE, kvw), bf),
            pltpu.VMEM((D, 8, 128), i32),
            pltpu.VMEM((table.shape[0], 128), i32),
            pltpu.SMEM((table.shape[0], 128), i32),
            pltpu.VMEM((requests, width * PAGE, kvw), bf),
            pltpu.VMEM((requests * heads, KVL + 128), f32),
            pltpu.VMEM((d1, fold, KVL + 128), f32),
            pltpu.VMEM((requests * heads, 128), f32),
            pltpu.VMEM((requests * heads, KVL), f32),
            pltpu.VMEM((D, fold, KVL), bf),
            dma((2,)), dma((2, D, K)), dma((D, K)), dma((g1, D, K)), dma((g1, D, K)),
            dma((t1, S)), dma((t1, S)), dma((s1,)), dma((s1,)), dma((l1,)), dma((l1,)),
            dma((t1, S)), dma((t1, S)), dma((s1,)), dma((s1,)), dma((l1,)), dma((l1,)),
            dma((d1,)), dma((d1,)), dma((d1,)), dma((d1,)),
            dma((d1,)), dma((d1,)), dma((d1,)), dma((d1,)),
        ],
        compiler_params=pltpu.CompilerParams(
            collective_id=0, has_side_effects=True, vmem_limit_bytes=56 * 1024 * 1024
        ),
    )(
        weight, hidden_x, qg, kv_gain[None, :], cosine, sine, source_ids, table,
        split_lens[:, 0], plan, want, old_cache, dec_query, new_key,
    )
    return q_out, a_out.reshape(requests, heads, KVL)


def body(
    hidden_x,
    proj_weight,
    q_gain,
    kv_gain,
    old_cache,
    page_plan,
    block_table,
    split_lens,
    dec_query,
    new_key,
):
    if fused_ok(hidden_x, proj_weight, dec_query, page_plan):
        return fused(
            hidden_x, proj_weight, q_gain, kv_gain, old_cache, page_plan, block_table,
            split_lens, dec_query, new_key,
        )
    projected = jnp.dot(
        hidden_x,
        lax.all_gather(proj_weight, "dec", axis=1, tiled=True),
        preferred_element_type=jnp.float32,
    )
    query_part = projected[:, :QL]
    kv_part = projected[:, QL:]
    tokens_here = hidden_x.shape[0]
    positions = (
        lax.axis_index("dec") * tokens_here + jnp.arange(tokens_here, dtype=jnp.int32)
    ).astype(jnp.float32)
    lane_count = lax.axis_size(("stg", "tp"))
    lane_index = lax.axis_index(("stg", "tp"))
    owner_count = lax.axis_size("dec")
    page_count = page_plan.shape[0]
    capacity = max(2, -(-page_count // owner_count))
    query_width = QL // lane_count
    query_cols, kv_cols = (
        lax.psum_scatter(query_part, ("stg", "tp"), scatter_dimension=1, tiled=True),
        lax.psum_scatter(kv_part, ("stg", "tp"), scatter_dimension=1, tiled=True),
    )
    kv_width = kv_cols.shape[1]
    col_start = lane_index * kv_width
    columns = col_start + jnp.arange(kv_width, dtype=jnp.int32)
    latent_part_sq = jnp.sum(jnp.where(columns[None, :] < KVL, kv_cols * kv_cols, 0.0), axis=1)
    query_sq, latent_sq = lax.psum(
        (jnp.sum(query_cols * query_cols, axis=1), latent_part_sq), ("stg", "tp")
    )
    kv_rows = kv_finish(kv_cols, col_start, latent_sq, kv_gain, positions)
    kv_pages = kv_rows.reshape(page_count, PAGE, kv_width)
    send_pages, send_labels = pack_pages(kv_pages, page_plan, owner_count, capacity)
    got_slices, got_labels = (
        lax.all_to_all(send_pages, "dec", split_axis=0, concat_axis=0, tiled=True),
        lax.all_to_all(send_labels, "dec", split_axis=0, concat_axis=0, tiled=True),
    )
    got_pages = lax.all_gather(got_slices, ("stg", "tp"), axis=3, tiled=True)
    query_gain = lax.dynamic_slice_in_dim(q_gain, lane_index * query_width, query_width)
    q_latent = (
        query_cols * lax.rsqrt(query_sq / QL + norm_eps)[:, None] * query_gain[None, :]
    ).astype(jnp.bfloat16)
    cache = place_pages(old_cache, got_pages, got_labels)
    slot_table = block_table[0]
    request_count = slot_table.shape[0]
    key_rows = jnp.take(cache, slot_table.reshape(-1), axis=0).reshape(
        request_count, -1, cache.shape[2]
    )
    scores = (
        jnp.einsum("rhc,rlc->rhl", dec_query, key_rows, preferred_element_type=jnp.float32)
        * softmax_scale
    )
    live_mask = jnp.arange(key_rows.shape[1], dtype=jnp.int32)[None, :] < split_lens[:, 0][:, None]
    scores = jnp.where(live_mask[:, None, :], scores, -1e30)
    row_peak = jnp.max(scores, axis=2)
    weights = jnp.where(live_mask[:, None, :], jnp.exp(scores - row_peak[:, :, None]), 0.0)
    row_total = jnp.sum(weights, axis=2)
    rounded = weights.astype(jnp.bfloat16)
    partial_out = jnp.einsum(
        "rhl,rlc->rhc", rounded, key_rows[:, :, :KVL], preferred_element_type=jnp.float32
    )
    peak_all, total_all, output_all = combined_all(
        (row_peak, row_total, partial_out), "dec", combine_parts
    )
    self_score = (
        jnp.einsum("rhc,rc->rh", dec_query, new_key, preferred_element_type=jnp.float32)
        * softmax_scale
    )
    overall = jnp.maximum(peak_all, self_score)
    carried = jnp.exp(peak_all - overall)
    self_weight = jnp.exp(self_score - overall)
    denom = total_all * carried + self_weight
    numer = output_all * carried[:, :, None] + self_weight[:, :, None] * new_key[
        :, None, :KVL
    ].astype(jnp.float32)
    attn_latent = (numer / denom[:, :, None]).astype(jnp.bfloat16)
    return (q_latent, attn_latent)


def solution(mesh):
    return jax.shard_map(
        body,
        mesh=mesh,
        in_specs=(
            P(("grp", "dec"), ("stg", "tp")),
            P(("stg", "tp"), "dec"),
            P(),
            P(),
            P(("grp", "dec"), None, None),
            P(("grp", "dec"), None),
            P(("grp", "dec"), None, None),
            P("grp", "dec"),
            P("grp", ("stg", "tp"), None),
            P("grp", None),
        ),
        out_specs=(P(("grp", "dec"), ("stg", "tp")), P("grp", ("stg", "tp"), None)),
        check_vma=False,
    )
```

```python
import functools

import jax
import jax.numpy as jnp
from jax import lax
from jax.experimental import pallas as pl
from jax.experimental.pallas import tpu as pltpu
from jax.sharding import PartitionSpec as P

QL = 1536
KVL = 512
ROPE = 64
PAGE = 32


softmax_scale = 192.0 ** (-0.5)
norm_eps = 1e-06


def combined_all(part, axis, combine):
    gathered = jax.tree.map(lambda a: lax.all_gather(a, axis), part)

    def take(source):
        return jax.tree.map(lambda a: lax.dynamic_index_in_dim(a, source, 0, False), gathered)

    return lax.fori_loop(
        1, lax.axis_size(axis), lambda source, state: combine(state, take(source)), take(0)
    )


def rope_rotate(matrix, col_start, positions):
    col_count = matrix.shape[1]
    columns = col_start + jnp.arange(col_count, dtype=jnp.int32)
    is_rope = columns >= KVL
    pair_index = jnp.maximum(columns - KVL, 0) // 2
    frequency = jnp.power(jnp.float32(10000.0), -(2 * pair_index).astype(jnp.float32) / ROPE)
    angles = positions[:, None] * frequency[None, :]
    cosine = jnp.where(is_rope[None, :], jnp.cos(angles), 1.0)
    sine_part = jnp.where(is_rope[None, :], jnp.sin(angles), 0.0)
    paired = matrix.reshape(matrix.shape[0], col_count // 2, 2)
    partner = jnp.stack([-paired[:, :, 1], paired[:, :, 0]], axis=2).reshape(matrix.shape)
    return matrix * cosine + partner * sine_part


def kv_finish(matrix, col_start, latent_sq, kv_gain, positions):
    col_count = matrix.shape[1]
    columns = col_start + jnp.arange(col_count, dtype=jnp.int32)
    gain_full = jnp.concatenate([kv_gain, jnp.ones((ROPE,), jnp.float32)])
    gain_cols = lax.dynamic_slice_in_dim(gain_full, col_start, col_count)
    inverse = lax.rsqrt(latent_sq / KVL + norm_eps)
    row_scale = jnp.where(columns[None, :] < KVL, inverse[:, None] * gain_cols[None, :], 1.0)
    return rope_rotate(matrix * row_scale, col_start, positions).astype(jnp.bfloat16)


def pack_pages(kv_pages, page_table, owner_count, capacity):
    owners = page_table[:, 0]
    slot_ids = page_table[:, 1]
    page_ids = jnp.arange(kv_pages.shape[0], dtype=jnp.int32)
    earlier = (owners[:, None] == owners[None, :]) & (page_ids[None, :] < page_ids[:, None])
    ranking = jnp.sum(earlier.astype(jnp.int32), axis=1)
    targets = owners * capacity + ranking
    places = jnp.arange(owner_count * capacity, dtype=jnp.int32)
    matches = targets[None, :] == places[:, None]
    source_ids = jnp.sum(jnp.where(matches, page_ids[None, :], 0), axis=1)
    filled = jnp.any(matches, axis=1)
    chosen = jnp.where(
        filled[:, None, None], jnp.take(kv_pages, source_ids, axis=0), jnp.zeros((), kv_pages.dtype)
    )
    labels = jnp.where(filled, jnp.take(slot_ids, source_ids), -1).astype(jnp.bfloat16)
    return (
        chosen.reshape(owner_count, capacity, kv_pages.shape[1], kv_pages.shape[2]),
        labels.reshape(owner_count, capacity),
    )


def place_pages(old_cache, got_pages, got_labels):
    flat_pages = got_pages.reshape(-1, old_cache.shape[1], old_cache.shape[2])
    label_ids = got_labels.reshape(-1).astype(jnp.int32)
    slot_ids = jnp.arange(old_cache.shape[0], dtype=jnp.int32)
    arrival_ids = jnp.arange(label_ids.shape[0], dtype=jnp.int32)
    matches = label_ids[None, :] == slot_ids[:, None]
    source_ids = jnp.sum(jnp.where(matches, arrival_ids[None, :], 0), axis=1)
    arrived = jnp.any(matches, axis=1)
    return jnp.where(arrived[:, None, None], jnp.take(flat_pages, source_ids, axis=0), old_cache)


def combine_parts(former, latter):
    overall = jnp.maximum(former[0], latter[0])
    front_scale = jnp.exp(former[0] - overall)
    back_scale = jnp.exp(latter[0] - overall)
    return (
        overall,
        former[1] * front_scale + latter[1] * back_scale,
        former[2] * front_scale[:, :, None] + latter[2] * back_scale[:, :, None],
    )


MESH = pl.DeviceIdType.MESH


def fused_kernel(
    dims, w_ref, x_ref, qg_ref, kg_ref, cos_ref, sin_ref, src_ref, bt_ref, lens_ref,
    plan_ref, want_ref, old_ref, dq_ref, nk_ref, q_out, a_out,
    wbuf, pt, aq, bq, cq, eq, ss, ssin, kvp, bk, ck, ek, kvl, sendp, got, plans,
    found, found_s, kbuf, part, parts, selfs, newk, fin,
    local_sem, zsem, zrecv, ysem, yrecv, t_send, t_recv, s_send, s_recv, v_send, v_recv,
    tk_send, tk_recv, sk_send, sk_recv, l_send, l_recv, pl_send, pl_recv, pg_send, pg_recv,
    c_send, c_recv, f_send, f_recv,
):
    D, G, S, T, K = dims
    C, fg = w_ref.shape[1], w_ref.shape[2]
    qw = q_out.shape[1]
    rows, kvw = kvp.shape
    lane_rows = rows // (S * T)
    chunk_rows = C // K
    cap = sendp.shape[1]
    requests, spans = kbuf.shape[0], kbuf.shape[1]
    table_width = spans // PAGE
    fold = part.shape[0] // D
    me, g = lax.axis_index("dec"), lax.axis_index("grp")
    st, tp = lax.axis_index("stg"), lax.axis_index("tp")
    lane = st * T + tp
    lane_steps = [(a, b) for a in range(S) for b in range(T) if a or b]

    def lane_at(a, b):
        return {"stg": lax.rem(st + a, S), "tp": lax.rem(tp + b, T)}

    def remote(src, dst, send, recv, target):
        return pltpu.make_async_remote_copy(
            src_ref=src, dst_ref=dst, send_sem=send, recv_sem=recv,
            device_id=target, device_id_type=MESH,
        )

    own = pltpu.make_async_copy(
        w_ref, wbuf.at[:, pl.ds(pl.multiple_of(me * C, 16), C)], local_sem.at[0]
    )
    own.start()
    barrier = pltpu.get_barrier_semaphore()
    greeted = [{"dec": lax.rem(me + d, D)} for d in range(1, D)]
    greeted += [{"grp": lax.rem(g + d, G)} for d in range(1, G)]
    greeted += [lane_at(a, b) for a, b in lane_steps]
    for target in greeted:
        pl.semaphore_signal(barrier, inc=1, device_id=target, device_id_type=MESH)
    pl.semaphore_wait(barrier, len(greeted))

    def chunk(j, half, c):
        start = pl.multiple_of(j * C + c * chunk_rows, 16)
        return wbuf.at[half, pl.ds(start, chunk_rows)]

    def z_copy(j, c, way, mine):
        src = w_ref.at[g, pl.ds(c * chunk_rows, chunk_rows)] if mine else chunk(j, g, c)
        to = me + 1 if way == 0 else me - 1
        return remote(src, chunk(j, g, c), zsem.at[way, j, c], zrecv.at[j, c], {"dec": to})

    def y_copy(j, c, d):
        return remote(
            chunk(j, g, c), chunk(j, g, c), ysem.at[d - 1, j, c], yrecv.at[d - 1, j, c],
            {"grp": lax.rem(g + d, G)},
        )

    def y_arrive(j, c, d):
        half = lax.rem(g + G - d, G)
        return remote(
            chunk(j, half, c), chunk(j, half, c), ysem.at[d - 1, j, c],
            yrecv.at[d - 1, j, c], {"grp": half},
        )

    def own_left(turn, c):
        @pl.when((me > 0) & (me == D - 1 - turn))
        def _():
            if turn > 0 and c < K - 2:
                z_copy(me, c + 2, 1, True).wait_send()
            z_copy(me, c, 1, True).start()

    plan_copies = []
    plans[me] = plan_ref[...]
    for d in range(1, D):
        copy = remote(
            plan_ref, plans.at[me], pl_send.at[d - 1], pl_recv.at[d - 1],
            {"dec": lax.rem(me + d, D)},
        )
        copy.start()
        plan_copies.append(copy)
    for c in reversed(range(K)):
        own_left(0, c)

    @pl.when(me < D - 1)
    def _():
        for c in reversed(range(K)):
            z_copy(me, c, 0, True).start()

    own.wait()

    def project(j):
        @pl.when(j * C < QL)
        def _():
            block = pl.ds(pl.multiple_of(j * C, 16), C)
            total = None
            for half in range(G):
                term = lax.dot_general(
                    wbuf[half, block, :], x_ref[:, half * fg : (half + 1) * fg],
                    (((1,), (1,)), ((), ())), preferred_element_type=jnp.float32,
                )
                total = term if total is None else total + term
            pt[block, :] = total

    project(me)

    def is_kv(j, c):
        return j * C + (c + 1) * chunk_rows > QL

    def finish_block(j, there):
        for c in range(K):
            @pl.when(there & jnp.logical_not(is_kv(j, c)))
            def _():
                for d in range(1, G):
                    y_arrive(j, c, d).wait_recv()

        @pl.when(there)
        def _():
            project(j)

    def relay(n):
        turn, c = n // K, K - 1 - n % K
        jr, jl = me - 1 - turn, D - 1 - turn
        if turn > 0:
            own_left(turn, c)

        @pl.when(jl > me)
        def _():
            z_copy(jl, c, 1, False).wait_recv()

            @pl.when(me > 0)
            def _():
                z_copy(jl, c, 1, False).start()
            for d in range(1, G):
                y_copy(jl, c, d).start()

        @pl.when(jr >= 0)
        def _():
            z_copy(jr, c, 0, False).wait_recv()

            @pl.when(me < D - 1)
            def _():
                z_copy(jr, c, 0, False).start()

            @pl.when(me == D - 1)
            def _():
                for d in range(1, G):
                    y_copy(jr, c, d).start()
        if turn > 0:
            @pl.when((me < D - 1) & (jr + 1 >= 0))
            def _():
                for d in range(1, G):
                    y_copy(jr + 1, c, d).start()

    tk, sk, lk, pg, cc, ff = [], [], [], [], [], []

    def k_rows(at):
        return kvp.at[pl.ds(pl.multiple_of(at * lane_rows, 16), lane_rows)]

    def kv_project():
        for j in range(D):
            for c in range(K):
                if is_kv(j, c):
                    @pl.when(me != j)
                    def _():
                        for d in range(1, G):
                            y_arrive(j, c, d).wait_recv()
        total = None
        for half in range(G):
            term = lax.dot_general(
                x_ref[:, half * fg : (half + 1) * fg], wbuf[half, QL:, :],
                (((1,), (1,)), ((), ())), preferred_element_type=jnp.float32,
            )
            total = term if total is None else total + term
        kvp[...] = total
        for d in range(1, T):
            t2 = lax.rem(tp + d, T)
            for a in range(S):
                copy = remote(
                    k_rows(a * T + t2), bk.at[d - 1, a], tk_send.at[d - 1, a],
                    tk_recv.at[d - 1, a], {"tp": t2},
                )
                copy.start()
                tk.append(copy)

    def kv_tp(a):
        k = k_rows(a * T + tp)[...]
        for d in range(T - 1):
            k = k + bk[d, a]
        return k

    def kv_across():
        for copy in tk:
            copy.wait_recv()
        for d in range(1, S):
            s2 = lax.rem(st + d, S)
            ck[d - 1] = kv_tp(s2)
            copy = remote(
                ck.at[d - 1], ek.at[d - 1], sk_send.at[d - 1], sk_recv.at[d - 1], {"stg": s2}
            )
            copy.start()
            sk.append(copy)

    def kv_norm():
        for copy in sk:
            copy.wait_recv()
        k = kv_tp(st)
        for d in range(S - 1):
            k = k + ek[d]
        lat, tail = k[:, :KVL], k[:, KVL:]
        square = jnp.sum(lat * lat, axis=1, keepdims=True)
        lat = lat * (lax.rsqrt(square / KVL + norm_eps) * kg_ref[...])
        to = lax.broadcasted_iota(jnp.int32, (ROPE, ROPE), 1)
        at = lax.broadcasted_iota(jnp.int32, (ROPE, ROPE), 0)
        even = lax.rem(to, 2) == 0
        swap = jnp.where(even & (at == to + 1), -1.0, 0.0)
        swap = jnp.where(jnp.logical_not(even) & (at == to - 1), 1.0, swap)
        partner = jnp.dot(
            tail, swap, preferred_element_type=jnp.float32, precision=lax.Precision.HIGHEST
        )
        tail = tail * cos_ref[...] + partner * sin_ref[...]
        pages = lane_rows // PAGE
        mine = pl.ds(lane * pages, pages)
        kvl[mine, :, :KVL] = lat.astype(jnp.bfloat16).reshape(pages, PAGE, KVL)
        kvl[mine, :, KVL:] = tail.astype(jnp.bfloat16).reshape(pages, PAGE, ROPE)
        for i, (a, b) in enumerate(lane_steps):
            copy = remote(
                kvl.at[mine], kvl.at[mine], l_send.at[i], l_recv.at[i], lane_at(a, b)
            )
            copy.start()
            lk.append(copy)
        for copy in plan_copies:
            copy.wait_recv()
        total = jnp.zeros(want_ref.shape, jnp.int32)
        for d in range(D):
            keys, ranks = plans[d, 0:1, :], plans[d, 1:2, :]
            total = total + jnp.where(keys == want_ref[...], d * cap + ranks + 1, 0)
        found[...] = jnp.broadcast_to(jnp.sum(total, axis=1, keepdims=True), found.shape)
        copy = pltpu.make_async_copy(found, found_s, local_sem.at[1])
        copy.start()
        copy.wait()

    def send_pages():
        for copy in lk:
            copy.wait_recv()
        for o in range(D):
            for r in range(cap):
                sendp[o, r] = kvl[src_ref[o * cap + r]]
        for d in range(1, D):
            to = lax.rem(me + d, D)
            copy = remote(
                sendp.at[to], got.at[me], pg_send.at[d - 1], pg_recv.at[d - 1], {"dec": to}
            )
            copy.start()
            pg.append(copy)
        got[me] = sendp[me]
        for r in range(requests):
            query = dq_ref[r].astype(jnp.float32)
            row = nk_ref[pl.ds(r, 1), :].astype(jnp.float32)
            score = jnp.sum(query * row, axis=1, keepdims=True) * softmax_scale
            heads = query.shape[0]
            selfs[r * heads : (r + 1) * heads, :] = jnp.broadcast_to(score, (heads, 128))
            newk[r * heads : (r + 1) * heads, :] = jnp.broadcast_to(row[:, :KVL], (heads, KVL))

    def attend():
        for copy in pg:
            copy.wait_recv()
        for r in range(requests):
            for j in range(table_width):
                place = r * table_width + j
                index = found_s[place, 0]
                came = jnp.clip(index - 1, 0, D * cap - 1)
                fresh = got[came // cap, lax.rem(came, cap)].astype(jnp.float32)
                stale = old_ref[bt_ref[place]].astype(jnp.float32)
                page = jnp.where(jnp.full(fresh.shape, index, jnp.int32) > 0, fresh, stale)
                kbuf[r, j * PAGE : (j + 1) * PAGE, :] = page.astype(jnp.bfloat16)
        for r in range(requests):
            scores = lax.dot_general(
                dq_ref[r], kbuf[r], (((1,), (1,)), ((), ())), preferred_element_type=jnp.float32
            ) * softmax_scale
            live = lax.broadcasted_iota(jnp.int32, scores.shape, 1) < lens_ref[r]
            scores = jnp.where(live, scores, -1e30)
            peak = jnp.max(scores, axis=1, keepdims=True)
            weight = jnp.where(live, jnp.exp(scores - peak), 0.0)
            total = jnp.sum(weight, axis=1, keepdims=True)
            heads = scores.shape[0]
            at = pl.ds(r * heads, heads)
            part[at, :KVL] = jnp.dot(
                weight.astype(jnp.bfloat16), kbuf[r, :, :KVL], preferred_element_type=jnp.float32
            )
            column = lax.broadcasted_iota(jnp.int32, (heads, 128), 1)
            part[at, KVL:] = jnp.where(column < 64, peak, total)
        for d in range(1, D):
            to = lax.rem(me + d, D)
            copy = remote(
                part.at[pl.ds(pl.multiple_of(to * fold, 8), fold)], parts.at[d - 1],
                c_send.at[d - 1], c_recv.at[d - 1], {"dec": to},
            )
            copy.start()
            cc.append(copy)

    def combine():
        for copy in cc:
            copy.wait_recv()
        mine = pl.ds(pl.multiple_of(me * fold, 8), fold)
        shares = [part[mine, :]] + [parts[d] for d in range(D - 1)]
        own_score = selfs[mine, 0:1]
        top = own_score
        for share in shares:
            top = jnp.maximum(top, share[:, KVL : KVL + 1])
        own_weight = jnp.exp(own_score - top)
        numer, denom = own_weight * newk[mine, :], own_weight
        for share in shares:
            factor = jnp.exp(share[:, KVL : KVL + 1] - top)
            numer = numer + factor * share[:, :KVL]
            denom = denom + factor * share[:, KVL + 64 : KVL + 65]
        fin[me] = (numer / denom).astype(jnp.bfloat16)
        for d in range(1, D):
            copy = remote(
                fin.at[me], fin.at[me], f_send.at[d - 1], f_recv.at[d - 1],
                {"dec": lax.rem(me + d, D)},
            )
            copy.start()
            ff.append(copy)

    items = K * (D - 1)
    kv_items = -(-kvw // chunk_rows)
    stages = [kv_project, kv_across, kv_norm, send_pages]
    first = min(kv_items + 3, items - 1)
    gaps = (0, 2, 6, 10)
    due = {}
    for gap, stage in zip(gaps, stages):
        due.setdefault(min(first + gap, items - 1), []).append(stage)
    for n in range(items):
        relay(n)
        if n > first and n % K == (first + 1) % K:
            turn = n // K - 1
            finish_block(me - 1 - turn, (me - 1 - turn >= 0) & (me == D - 1))
            if turn > 0:
                finish_block(me - turn, (me - turn >= 0) & (me < D - 1))
            finish_block(jnp.int32(D - 1 - turn), D - 1 - turn > me)
        for stage in due.get(n, ()):
            stage()
    turn = D - 2
    finish_block(me - 1 - turn, (me - 1 - turn >= 0) & (me == D - 1))
    finish_block(me - turn, (me - turn >= 0) & (me < D - 1))
    finish_block(jnp.int32(D - 1 - turn), D - 1 - turn > me)

    def q_rows(at):
        return pt[pl.ds(pl.multiple_of(at * qw, 16), qw), :]

    near = []
    for i in range(1, S + 1):
        a = lax.rem(st + i, S)
        group = []
        for d in range(1, T):
            t2 = lax.rem(tp + d, T)
            aq[d - 1, a] = q_rows(a * T + t2).astype(jnp.bfloat16)
            copy = remote(
                aq.at[d - 1, a], bq.at[d - 1, a], t_send.at[d - 1, a], t_recv.at[d - 1, a],
                {"tp": t2},
            )
            copy.start()
            group.append(copy)
        near.append(group)
    attend()

    def q_tp(a):
        q = q_rows(a * T + tp)
        for d in range(T - 1):
            q = q + bq[d, a].astype(jnp.float32)
        return q

    far = []
    for d in range(1, S):
        s2 = lax.rem(st + d, S)
        for copy in near[d - 1]:
            copy.wait_recv()
        cq[d - 1] = q_tp(s2).astype(jnp.bfloat16)
        copy = remote(
            cq.at[d - 1], eq.at[d - 1], s_send.at[d - 1], s_recv.at[d - 1], {"stg": s2}
        )
        copy.start()
        far.append(copy)
    for copy in near[S - 1]:
        copy.wait_recv()
    q = q_tp(st)
    combine()
    for copy in far:
        copy.wait_recv()
    for d in range(S - 1):
        q = q + eq[d].astype(jnp.float32)
    ss[...] = jnp.broadcast_to(jnp.sum(q * q, axis=0, keepdims=True), ss.shape)
    small = []
    for i, (a, b) in enumerate(lane_steps):
        copy = remote(ss, ssin.at[i], v_send.at[i], v_recv.at[i], lane_at(a, b))
        copy.start()
        small.append(copy)
    square = ss[...]
    for copy in ff:
        copy.wait_recv()
    for e in range(D):
        a_out[e * fold : (e + 1) * fold, :] = fin[e]
    for i, copy in enumerate(small):
        copy.wait_recv()
        square = square + ssin[i]
    q = jnp.transpose(q * lax.rsqrt(square[0:1] / QL + norm_eps))
    gain = qg_ref[:, pl.ds(pl.multiple_of(lane * qw, 128), qw)]
    q_out[...] = (q * gain).astype(jnp.bfloat16)

    for copy in plan_copies + tk + sk + lk + pg + cc + ff + sum(near, []) + far + small:
        copy.wait_send()
    for c in range(K):
        @pl.when((me > 0) if c < 2 else (me == D - 1))
        def _():
            z_copy(me, c, 1, True).wait_send()

        @pl.when(me < D - 1)
        def _():
            z_copy(me, c, 0, True).wait_send()
        for j in range(D):
            @pl.when((j > me) & (me > 0))
            def _():
                z_copy(j, c, 1, False).wait_send()

            @pl.when((j < me) & (me < D - 1))
            def _():
                z_copy(j, c, 0, False).wait_send()

            @pl.when(j != me)
            def _():
                for d in range(1, G):
                    y_copy(j, c, d).wait_send()


def chunk_count(rows):
    return next((k for k in (11, 3, 2) if rows % (16 * k) == 0), 1)


def fused_ok(hidden_x, proj_weight, dec_query, page_plan):
    D, G, S, T = [lax.axis_size(n) for n in ("dec", "grp", "stg", "tp")]
    lanes, columns = S * T, proj_weight.shape[1]
    return (
        D > 2
        and chunk_count(columns) > 5
        and columns % 16 == 0
        and (D - 2) * columns <= QL
        and hidden_x.shape[0] % 128 == 0
        and hidden_x.shape[0] % (PAGE * lanes) == 0
        and hidden_x.shape[1] % (128 * G) == 0
        and QL % (128 * lanes) == 0
        and dec_query.shape[1] % 16 == 0
        and dec_query.shape[0] * dec_query.shape[1] % (16 * D) == 0
        and page_plan.shape[0] <= 128
    )


def fused(
    hidden_x, proj_weight, q_gain, kv_gain, old_cache, page_plan, block_table, split_lens,
    dec_query, new_key,
):
    D, G, S, T = [lax.axis_size(n) for n in ("dec", "grp", "stg", "tp")]
    L = S * T
    rows, features = hidden_x.shape
    C = proj_weight.shape[1]
    K = chunk_count(C)
    fg, qw, kvw = features // G, QL // L, KVL + ROPE
    lane, me = lax.axis_index(("stg", "tp")), lax.axis_index("dec")
    lane_rows = rows // L
    weight = jnp.transpose(proj_weight.reshape(G, fg, C), (0, 2, 1))
    qg = q_gain[None, :]
    positions = (
        me * rows + lane * lane_rows + jnp.arange(lane_rows, dtype=jnp.int32)
    ).astype(jnp.float32)
    pair_index = jnp.arange(ROPE, dtype=jnp.int32) // 2
    frequency = jnp.power(jnp.float32(10000.0), -(2 * pair_index).astype(jnp.float32) / ROPE)
    angles = positions[:, None] * frequency[None, :]
    cosine, sine = jnp.cos(angles), jnp.sin(angles)

    pages, slots = page_plan.shape[0], old_cache.shape[0]
    cap = max(2, -(-pages // D))
    owners = page_plan[:, 0]
    page_ids = jnp.arange(pages, dtype=jnp.int32)
    earlier = (owners[:, None] == owners[None, :]) & (page_ids[None, :] < page_ids[:, None])
    ranking = jnp.sum(earlier.astype(jnp.int32), axis=1)
    places = jnp.arange(D * cap, dtype=jnp.int32)
    matches = (owners * cap + ranking)[None, :] == places[:, None]
    source_ids = jnp.sum(jnp.where(matches, page_ids[None, :], 0), axis=1)
    plan = jnp.stack([owners * slots + page_plan[:, 1], ranking])
    plan = jnp.pad(plan, ((0, 6), (0, 128 - pages)), constant_values=-1)
    table = block_table.reshape(-1)
    want = jnp.broadcast_to((me * slots + table)[:, None], (table.shape[0], 128))
    requests, heads = dec_query.shape[0], dec_query.shape[1]
    width = block_table.shape[2]
    fold = requests * heads // D
    dma = pltpu.SemaphoreType.DMA
    bf, f32, i32 = jnp.bfloat16, jnp.float32, jnp.int32
    t1, s1, g1, l1, d1 = max(T - 1, 1), max(S - 1, 1), max(G - 1, 1), max(L - 1, 1), D - 1
    vmem = pl.BlockSpec(memory_space=pltpu.VMEM)
    smem = pl.BlockSpec(memory_space=pltpu.SMEM)
    q_out, a_out = pl.pallas_call(
        functools.partial(fused_kernel, (D, G, S, T, K)),
        out_shape=(
            jax.ShapeDtypeStruct((rows, qw), bf),
            jax.ShapeDtypeStruct((requests * heads, KVL), bf),
        ),
        in_specs=[vmem] * 6 + [smem] * 3 + [vmem] * 5,
        out_specs=(vmem, vmem),
        scratch_shapes=[
            pltpu.VMEM((G, D * C, fg), bf),
            pltpu.VMEM((D * C, rows), f32),
            pltpu.VMEM((t1, S, qw, rows), bf),
            pltpu.VMEM((t1, S, qw, rows), bf),
            pltpu.VMEM((s1, qw, rows), bf),
            pltpu.VMEM((s1, qw, rows), bf),
            pltpu.VMEM((8, rows), f32),
            pltpu.VMEM((l1, 8, rows), f32),
            pltpu.VMEM((rows, kvw), f32),
            pltpu.VMEM((t1, S, lane_rows, kvw), f32),
            pltpu.VMEM((s1, lane_rows, kvw), f32),
            pltpu.VMEM((s1, lane_rows, kvw), f32),
            pltpu.VMEM((pages, PAGE, kvw), bf),
            pltpu.VMEM((D, cap, PAGE, kvw), bf),
            pltpu.VMEM((D, cap, PAGE, kvw), bf),
            pltpu.VMEM((D, 8, 128), i32),
            pltpu.VMEM((table.shape[0], 128), i32),
            pltpu.SMEM((table.shape[0], 128), i32),
            pltpu.VMEM((requests, width * PAGE, kvw), bf),
            pltpu.VMEM((requests * heads, KVL + 128), f32),
            pltpu.VMEM((d1, fold, KVL + 128), f32),
            pltpu.VMEM((requests * heads, 128), f32),
            pltpu.VMEM((requests * heads, KVL), f32),
            pltpu.VMEM((D, fold, KVL), bf),
            dma((2,)), dma((2, D, K)), dma((D, K)), dma((g1, D, K)), dma((g1, D, K)),
            dma((t1, S)), dma((t1, S)), dma((s1,)), dma((s1,)), dma((l1,)), dma((l1,)),
            dma((t1, S)), dma((t1, S)), dma((s1,)), dma((s1,)), dma((l1,)), dma((l1,)),
            dma((d1,)), dma((d1,)), dma((d1,)), dma((d1,)),
            dma((d1,)), dma((d1,)), dma((d1,)), dma((d1,)),
        ],
        compiler_params=pltpu.CompilerParams(
            collective_id=0, has_side_effects=True, vmem_limit_bytes=56 * 1024 * 1024
        ),
    )(
        weight, hidden_x, qg, kv_gain[None, :], cosine, sine, source_ids, table,
        split_lens[:, 0], plan, want, old_cache, dec_query, new_key,
    )
    return q_out, a_out.reshape(requests, heads, KVL)


def body(
    hidden_x,
    proj_weight,
    q_gain,
    kv_gain,
    old_cache,
    page_plan,
    block_table,
    split_lens,
    dec_query,
    new_key,
):
    if fused_ok(hidden_x, proj_weight, dec_query, page_plan):
        return fused(
            hidden_x, proj_weight, q_gain, kv_gain, old_cache, page_plan, block_table,
            split_lens, dec_query, new_key,
        )
    projected = jnp.dot(
        hidden_x,
        lax.all_gather(proj_weight, "dec", axis=1, tiled=True),
        preferred_element_type=jnp.float32,
    )
    query_part = projected[:, :QL]
    kv_part = projected[:, QL:]
    tokens_here = hidden_x.shape[0]
    positions = (
        lax.axis_index("dec") * tokens_here + jnp.arange(tokens_here, dtype=jnp.int32)
    ).astype(jnp.float32)
    lane_count = lax.axis_size(("stg", "tp"))
    lane_index = lax.axis_index(("stg", "tp"))
    owner_count = lax.axis_size("dec")
    page_count = page_plan.shape[0]
    capacity = max(2, -(-page_count // owner_count))
    query_width = QL // lane_count
    query_cols, kv_cols = (
        lax.psum_scatter(query_part, ("stg", "tp"), scatter_dimension=1, tiled=True),
        lax.psum_scatter(kv_part, ("stg", "tp"), scatter_dimension=1, tiled=True),
    )
    kv_width = kv_cols.shape[1]
    col_start = lane_index * kv_width
    columns = col_start + jnp.arange(kv_width, dtype=jnp.int32)
    latent_part_sq = jnp.sum(jnp.where(columns[None, :] < KVL, kv_cols * kv_cols, 0.0), axis=1)
    query_sq, latent_sq = lax.psum(
        (jnp.sum(query_cols * query_cols, axis=1), latent_part_sq), ("stg", "tp")
    )
    kv_rows = kv_finish(kv_cols, col_start, latent_sq, kv_gain, positions)
    kv_pages = kv_rows.reshape(page_count, PAGE, kv_width)
    send_pages, send_labels = pack_pages(kv_pages, page_plan, owner_count, capacity)
    got_slices, got_labels = (
        lax.all_to_all(send_pages, "dec", split_axis=0, concat_axis=0, tiled=True),
        lax.all_to_all(send_labels, "dec", split_axis=0, concat_axis=0, tiled=True),
    )
    got_pages = lax.all_gather(got_slices, ("stg", "tp"), axis=3, tiled=True)
    query_gain = lax.dynamic_slice_in_dim(q_gain, lane_index * query_width, query_width)
    q_latent = (
        query_cols * lax.rsqrt(query_sq / QL + norm_eps)[:, None] * query_gain[None, :]
    ).astype(jnp.bfloat16)
    cache = place_pages(old_cache, got_pages, got_labels)
    slot_table = block_table[0]
    request_count = slot_table.shape[0]
    key_rows = jnp.take(cache, slot_table.reshape(-1), axis=0).reshape(
        request_count, -1, cache.shape[2]
    )
    scores = (
        jnp.einsum("rhc,rlc->rhl", dec_query, key_rows, preferred_element_type=jnp.float32)
        * softmax_scale
    )
    live_mask = jnp.arange(key_rows.shape[1], dtype=jnp.int32)[None, :] < split_lens[:, 0][:, None]
    scores = jnp.where(live_mask[:, None, :], scores, -1e30)
    row_peak = jnp.max(scores, axis=2)
    weights = jnp.where(live_mask[:, None, :], jnp.exp(scores - row_peak[:, :, None]), 0.0)
    row_total = jnp.sum(weights, axis=2)
    rounded = weights.astype(jnp.bfloat16)
    partial_out = jnp.einsum(
        "rhl,rlc->rhc", rounded, key_rows[:, :, :KVL], preferred_element_type=jnp.float32
    )
    peak_all, total_all, output_all = combined_all(
        (row_peak, row_total, partial_out), "dec", combine_parts
    )
    self_score = (
        jnp.einsum("rhc,rc->rh", dec_query, new_key, preferred_element_type=jnp.float32)
        * softmax_scale
    )
    overall = jnp.maximum(peak_all, self_score)
    carried = jnp.exp(peak_all - overall)
    self_weight = jnp.exp(self_score - overall)
    denom = total_all * carried + self_weight
    numer = output_all * carried[:, :, None] + self_weight[:, :, None] * new_key[
        :, None, :KVL
    ].astype(jnp.float32)
    attn_latent = (numer / denom[:, :, None]).astype(jnp.bfloat16)
    return (q_latent, attn_latent)


def solution(mesh):
    return jax.shard_map(
        body,
        mesh=mesh,
        in_specs=(
            P(("grp", "dec"), ("stg", "tp")),
            P(("stg", "tp"), "dec"),
            P(),
            P(),
            P(("grp", "dec"), None, None),
            P(("grp", "dec"), None),
            P(("grp", "dec"), None, None),
            P("grp", "dec"),
            P("grp", ("stg", "tp"), None),
            P("grp", None),
        ),
        out_specs=(P(("grp", "dec"), ("stg", "tp")), P("grp", ("stg", "tp"), None)),
        check_vma=False,
    )
```
